256 devices in a mesh: var: 8 (over z), lon: 16 (over y_lo, x, core), lat: 2 (over y_hi).
Axes of the slice: x: 4, y: 4 (y_hi: 2, y_lo: 2; y = y_hi * 2 + y_lo), z: 8, core: 2. Of those that a mesh axis runs over, the one named last changes fastest.
Arguments:
- fields: bfloat16 [48, 2, 96, 192, 16], P(('var', 'lat'), None, None, 'lon'), may hold values from -6 to 6
- score_table: bfloat16 [48, 16, 8], replicated, may hold values from -120 to 120
- score_bias: float32 [48, 8], replicated, may hold values from -6 to 6
- value_table: bfloat16 [48, 16, 512], replicated, may hold values from -1.5 to 1.5
- value_bias: float32 [48, 512], replicated, may hold values from -6 to 6
- agg_weight: bfloat16 [512, 512], replicated, may hold values from -0.25 to 0.25
- qkv_weight: bfloat16 [2, 512, 1536], replicated, may hold values from -10 to 10
- proj_weight: bfloat16 [2, 512, 512], replicated, may hold values from -0.25 to 0.25
- up_weight: bfloat16 [512, 2048], replicated, may hold values from -0.25 to 0.25
- down_weight: bfloat16 [2048, 512], replicated, may hold values from -0.125 to 0.125
- norm_gains: float32 [4, 512], replicated, may hold values from 0.1 to 1.9
- decode_weight: bfloat16 [512, 768], replicated, may hold values from -0.25 to 0.25
- decode_bias: float32 [768], replicated, may hold values from -3 to 3
Outputs:
- forecast: bfloat16 [2, 96, 192, 768], P(None, ('var', 'lat'), 'lon')
The draws below stay inside these ranges and needn't reach their ends.
All inputs are finite; a program needn't handle non-finite values.
Results may differ from the reference program's by a relative error of at most 0.025.
Values may be sent and summed in bfloat16 or wider, within the bound.
A program may use at most 128 MiB of HBM per device.

```python
import math
import jax
import jax.numpy as jnp
from jax import lax

D = 512
FF = 2048
HEADS = 8
VARS = 48
PATCH = 16
LEV = 2
WLEV = 2
WLAT = 6
WLON = 12
BLOCKS = 2
LATS = 96
LONS = 192
N_VAR = 8
N_LAT = 2


def draw_score_table(key, part):
    base = jax.random.normal(key, (VARS, PATCH, HEADS), jnp.float32)
    drawn = jnp.clip(base * 0.5, -3.0, 3.0)
    return drawn.astype(jnp.bfloat16)


def draw_qkv_weight(key, part):
    base = jax.random.normal(key, (BLOCKS, D, 3 * D), jnp.float32) / math.sqrt(D)
    drawn = base
    return jnp.clip(drawn, -10.0, 10.0).astype(jnp.bfloat16)


def shard_levels(key, extent, split, least, largest):
    loudness = 1.0
    for dim, shards_of in split:
        draws = jax.random.uniform(jax.random.fold_in(jax.random.fold_in(key, 6), dim), (shards_of,), jnp.float32, least / len(split), largest / len(split))
        loudness = loudness * jnp.repeat(jnp.exp(draws), extent[dim] // shards_of).reshape((-1,) + (1,) * (len(extent) - 1 - dim))
    return loudness


def noise(stream_key, dims, scale, most, cuts=(), kind=jnp.bfloat16):
    level = shard_levels(stream_key, dims, cuts, -0.22, 0.18) if cuts else 1.0
    array = jax.random.normal(stream_key, dims, jnp.float32) * scale * level
    return jnp.minimum(jnp.maximum(array, -most), most).astype(kind)


def setup_inputs(seed: int = 0) -> dict:
    key_list = jax.random.split(jax.random.key(seed), 14)
    fields = noise(key_list[0], (VARS, LEV, LATS, LONS, PATCH), 1.0, 6.0, ((0, 16), (3, 16)))
    score_table = draw_score_table(jax.random.fold_in(key_list[13], 71), 0)
    score_bias = noise(key_list[2], (VARS, HEADS), 1.0, 6.0, (), jnp.float32)
    value_table = noise(key_list[3], (VARS, PATCH, D), PATCH ** -0.5, 1.5)
    value_bias = noise(key_list[4], (VARS, D), 1.0, 6.0, (), jnp.float32)
    agg_weight = noise(key_list[5], (D, D), D ** -0.5, 0.25)
    qkv_weight = draw_qkv_weight(jax.random.fold_in(key_list[13], 71), 0)
    proj_weight = noise(key_list[7], (BLOCKS, D, D), D ** -0.5, 0.25)
    up_weight = noise(key_list[8], (D, FF), D ** -0.5, 0.25)
    down_weight = noise(key_list[9], (FF, D), FF ** -0.5, 0.125)
    norm_gains = jnp.clip(1.0 + 0.18 * jax.random.normal(key_list[10], (4, D), jnp.float32), 0.1, 1.9)
    decode_weight = noise(key_list[11], (D, VARS * PATCH), D ** -0.5, 0.25)
    decode_bias = noise(key_list[12], (VARS * PATCH,), 0.5, 3.0, (), jnp.float32)
    return {"fields": fields, "score_table": score_table, "score_bias": score_bias, "value_table": value_table, "value_bias": value_bias, "agg_weight": agg_weight, "qkv_weight": qkv_weight, "proj_weight": proj_weight, "up_weight": up_weight, "down_weight": down_weight, "norm_gains": norm_gains, "decode_weight": decode_weight, "decode_bias": decode_bias}


EPSILON = 1e-05

def layer_norm(values, norm_gain):
    centre = lax.optimization_barrier(jnp.mean(values, axis=-1, keepdims=True))
    shifted = values - centre
    spread = lax.optimization_barrier(jnp.mean(shifted * shifted, axis=-1, keepdims=True))
    return shifted * lax.rsqrt(spread + EPSILON) * norm_gain

def group_terms(patches, scores, top_score, table, offsets):
    levels, rows, cols, patch_size = patches.shape[1:]
    head_count = scores.shape[-1]
    width = table.shape[-1]

    def add_var(totals, pieces):
        patch, score, tab, offset = pieces
        weights = jnp.exp(score - top_score)
        values = jnp.dot(patch.reshape(-1, patch_size), tab, preferred_element_type=jnp.float32) + offset
        values = values.reshape(levels, rows, cols, head_count, width // head_count)
        return ((totals[0] + weights[..., None] * values, totals[1] + weights), None)
    start = (jnp.zeros((levels, rows, cols, head_count, width // head_count), jnp.float32), jnp.zeros((levels, rows, cols, head_count), jnp.float32))
    sums, _ = lax.scan(add_var, start, (patches, scores, table, offsets))
    return sums

def attend(queries, keys_vals, allowed):
    windows, length, model_width = queries.shape
    head_dim = model_width // HEADS
    query_heads = queries.astype(jnp.float32).reshape(windows, length, HEADS, head_dim)
    key_heads = keys_vals[..., :model_width].astype(jnp.float32).reshape(windows, -1, HEADS, head_dim)
    value_heads = keys_vals[..., model_width:].astype(jnp.float32).reshape(windows, -1, HEADS, head_dim)
    scores = jnp.einsum('bqhd,bkhd->bhqk', query_heads, key_heads) / math.sqrt(head_dim)
    scores = jnp.where(allowed[:, None], scores, -jnp.inf)
    scores = scores - lax.optimization_barrier(jnp.max(scores, axis=-1, keepdims=True))
    raised = jnp.exp(scores)
    weights = (raised / lax.optimization_barrier(jnp.sum(raised, axis=-1, keepdims=True))).astype(jnp.bfloat16)
    context = jnp.einsum('bhqk,bkhd->bqhd', weights.astype(jnp.float32), value_heads)
    return context.astype(jnp.bfloat16).reshape(windows, length, model_width)

def to_windows(source, window_sizes):
    level_size, row_size, col_size = window_sizes
    level_count, row_count, col_count, features = source.shape
    blocked = source.reshape(level_count // level_size, level_size, row_count // row_size, row_size, col_count // col_size, col_size, features)
    blocked = blocked.transpose(0, 2, 4, 1, 3, 5, 6)
    return blocked.reshape(level_count // level_size, -1, level_size * row_size * col_size, features)

def from_windows(windowed, full_shape, window_sizes):
    level_size, row_size, col_size = window_sizes
    level_count, row_count, col_count, features = full_shape
    blocked = windowed.reshape(level_count // level_size, row_count // row_size, col_count // col_size, level_size, row_size, col_size, features)
    return blocked.transpose(0, 3, 1, 4, 2, 5, 6).reshape(full_shape)

def window_block(latent, norm_gain, qkv_part, proj_part, offsets):
    level_shift, row_shift, col_shift = offsets
    sizes = (WLEV, WLAT, WLON)
    normed = layer_norm(latent, norm_gain).astype(jnp.bfloat16)
    projected = jnp.dot(normed, qkv_part, preferred_element_type=jnp.float32).astype(jnp.bfloat16)
    level_ids = (jnp.arange(LEV) + level_shift) // WLEV
    row_ids = (jnp.arange(LATS) + row_shift) // WLAT
    col_ids = (jnp.arange(LONS) + col_shift) % LONS // WLON
    cell_ids = jnp.stack(jnp.broadcast_arrays(level_ids[:, None, None], row_ids[None, :, None], col_ids[None, None, :]), axis=-1)
    rolled = jnp.roll(projected, (-level_shift, -row_shift, -col_shift), axis=(0, 1, 2))
    rolled_ids = jnp.roll(cell_ids, (-level_shift, -row_shift, -col_shift), axis=(0, 1, 2))
    windowed = to_windows(rolled, sizes)
    window_ids = to_windows(rolled_ids, sizes)

    def one_level(pieces):
        block_qkv, block_ids = pieces
        allowed = jnp.all(block_ids[:, :, None, :] == block_ids[:, None, :, :], axis=-1)
        return attend(block_qkv[..., :D], block_qkv[..., D:], allowed)
    context = lax.map(one_level, (windowed, window_ids))
    context = from_windows(context, (LEV, LATS, LONS, D), sizes)
    context = jnp.roll(context, (level_shift, row_shift, col_shift), axis=(0, 1, 2))
    return latent + jnp.dot(context, proj_part, preferred_element_type=jnp.float32)

def reference(fields, score_table, score_bias, value_table, value_bias, agg_weight, qkv_weight, proj_weight, up_weight, down_weight, norm_gains, decode_weight, decode_bias):
    groups = N_VAR * N_LAT
    group_vars = VARS // groups
    head_dim = D // HEADS
    widened = fields.astype(jnp.float32)
    scores = jnp.einsum('vlrcp,vph->vlrch', widened, score_table.astype(jnp.float32)) + score_bias[:, None, None, None, :]
    top_score = lax.optimization_barrier(jnp.max(scores, axis=0))
    grouped_fields = fields.reshape(groups, group_vars, LEV, LATS, LONS, PATCH)
    grouped_scores = scores.reshape(groups, group_vars, LEV, LATS, LONS, HEADS)
    grouped_tables = value_table.reshape(groups, group_vars, PATCH, D)
    grouped_offsets = value_bias.reshape(groups, group_vars, D)

    def add_group(totals, pieces):
        field_part, score_part, table_part, offset_part = pieces
        numerator, denominator = group_terms(field_part, score_part, top_score, table_part, offset_part)
        numerator = lax.optimization_barrier(numerator.astype(jnp.bfloat16)).astype(jnp.float32)
        denominator = lax.optimization_barrier(denominator.astype(jnp.bfloat16)).astype(jnp.float32)
        return ((totals[0] + numerator, totals[1] + denominator), None)
    start = (jnp.zeros((LEV, LATS, LONS, HEADS, head_dim), jnp.float32), jnp.zeros((LEV, LATS, LONS, HEADS), jnp.float32))
    sums, _ = lax.scan(add_group, start, (grouped_fields, grouped_scores, grouped_tables, grouped_offsets))
    pooled = (sums[0] / sums[1][..., None]).reshape(LEV, LATS, LONS, D).astype(jnp.bfloat16)
    latent = jnp.dot(pooled, agg_weight, preferred_element_type=jnp.float32)
    hidden = window_block(latent, norm_gains[0], qkv_weight[0], proj_weight[0], (0, 0, 0))
    mixed = layer_norm(hidden, norm_gains[1]).astype(jnp.bfloat16)
    active = jax.nn.gelu(jnp.dot(mixed, up_weight, preferred_element_type=jnp.float32), approximate=True).astype(jnp.bfloat16)
    latent = hidden + jnp.dot(active, down_weight, preferred_element_type=jnp.float32)
    latent = window_block(latent, norm_gains[2], qkv_weight[1], proj_weight[1], (WLEV // 2, WLAT // 2, WLON // 2))
    final = layer_norm(latent, norm_gains[3]).astype(jnp.bfloat16)
    return (jnp.dot(final, decode_weight, preferred_element_type=jnp.float32) + decode_bias).astype(jnp.bfloat16)
```

```python
import functools

import jax
import jax.numpy as jnp
import numpy as np
from jax import lax
from jax.experimental import pallas as pl
from jax.experimental.pallas import tpu as pltpu
from jax.sharding import PartitionSpec as P

MESH = pl.DeviceIdType.MESH
EPSILON = 1e-05
F32 = jnp.float32
BF16 = jnp.bfloat16

GROUPS = 16
LONS = 16
LEV, ROWS, COLS = 2, 6, 12
CELLS = LEV * ROWS * COLS
LOCAL_VARS, PATCH, HEADS, HEAD_DIM = 3, 16, 8, 64
VARS = GROUPS * LOCAL_VARS
D, FF = 512, 2048
SLOT = 64
KDIM = GROUPS * SLOT
QUAD = 48
QUAD_CELLS = 36
SENT = 40


def cell_index(row, col, lev):
    return (row * COLS + col) * LEV + lev


def band_selector():
    out = np.zeros((GROUPS * 8, GROUPS * ROWS), np.float32)
    for band in range(GROUPS):
        for row in range(ROWS):
            out[band * 8 + row, band * ROWS + row] = 1
    return out


def cell_selector():
    out = np.zeros((CELLS, LEV * COLS * 8), np.float32)
    for lev in range(LEV):
        for col in range(COLS):
            for row in range(ROWS):
                out[cell_index(row, col, lev), (lev * COLS + col) * 8 + row] = 1
    return out


def quad_selector():
    out = np.zeros((4 * QUAD, CELLS), np.float32)
    for row in range(ROWS):
        for col in range(COLS):
            for lev in range(LEV):
                quad = (row // 3) * 2 + col // 6
                place = ((row % 3) * 6 + col % 6) * LEV + lev
                out[quad * QUAD + place, cell_index(row, col, lev)] = 1
    return out


def weight_spread():
    out = np.zeros((128, KDIM), np.float32)
    for group in range(GROUPS):
        for var in range(LOCAL_VARS):
            v, at = group * LOCAL_VARS + var, group * SLOT
            out[v, at + var * PATCH : at + (var + 1) * PATCH] = 1
            out[v, at + 48 + var] = 1
            out[v, at + 51 + var] = 1
    return out


def bias_rows():
    high = np.zeros((GROUPS * 8, VARS), np.float32)
    low = np.zeros((GROUPS * 8, VARS), np.float32)
    for group in range(GROUPS):
        for var in range(LOCAL_VARS):
            high[group * 8 + var, group * LOCAL_VARS + var] = 1
            low[group * 8 + 3 + var, group * LOCAL_VARS + var] = 1
    return high, low


def dot(a, b):
    return jnp.dot(a, b, preferred_element_type=F32)


def dot_t(a, b):
    return lax.dot_general(a, b, (((1,), (1,)), ((), ())), preferred_element_type=F32)


def layer_norm(values, gain):
    shifted = values - jnp.mean(values, axis=-1, keepdims=True)
    spread = jnp.mean(shifted * shifted, axis=-1, keepdims=True)
    return shifted * lax.rsqrt(spread + EPSILON) * gain


def lane_low(rows):
    return lax.broadcasted_iota(jnp.int32, (rows, 128), 1) < HEAD_DIM


def attention_pair(q, k, v, allowed):
    q_low, k_low = lane_low(q.shape[0]), lane_low(k.shape[0])
    total = None
    for low in (True, False):
        q_own = jnp.where(q_low == low, q, jnp.zeros_like(q))
        v_own = jnp.where(k_low == low, v, jnp.zeros_like(v))
        scores = dot_t(q_own, k) * (1.0 / 8.0)
        if allowed is not None:
            scores = jnp.where(allowed, scores, -jnp.inf)
        raised = jnp.exp(scores - jnp.max(scores, axis=-1, keepdims=True))
        probs = (raised * (1.0 / jnp.sum(raised, axis=-1, keepdims=True))).astype(BF16)
        part = dot(probs, v_own)
        total = part if total is None else total + part
    return total.astype(BF16)


def body(
    fields_ref,
    band_sel_ref,
    score_tab_ref,
    score_bias_ref,
    value_bias_ref,
    gains_ref,
    decode_bias_ref,
    high_ref,
    low_ref,
    ones_ref,
    cell_sel_hbm,
    quad_sel_hbm,
    quad_back_hbm,
    spread_hbm,
    value_tab_hbm,
    agg_hbm,
    qkv_hbm,
    proj_hbm,
    up_hbm,
    down_hbm,
    decode_hbm,
    out_ref,
    outgoing,
    incoming,
    cell_sel,
    quad_sel,
    quad_back,
    spread,
    table,
    agg,
    qkv_w,
    proj_w,
    up_w,
    down_w,
    decode_w,
    score_w,
    pool_in,
    pooled,
    normed_q,
    kv2,
    context,
    send_sem,
    recv_sem,
    halo_send,
    halo_recv,
    load_sem,
):
    var, lon, lat = lax.axis_index("var"), lax.axis_index("lon"), lax.axis_index("lat")
    band = var * 2 + lat
    up_band, down_band = lax.rem(band + GROUPS - 1, GROUPS), lax.rem(band + 1, GROUPS)
    left, right = lax.rem(lon + LONS - 1, LONS), lax.rem(lon + 1, LONS)

    def device(of_band, of_lon):
        return (of_band // 2, of_lon, lax.rem(of_band, 2))

    barrier = pltpu.get_barrier_semaphore()
    peers = [device(lax.rem(band + k, GROUPS), lon) for k in range(1, GROUPS)]
    peers += [device(b, c) for b in (band, up_band, down_band) for c in (left, right)]
    for peer in peers:
        pl.semaphore_signal(barrier, inc=1, device_id=peer, device_id_type=MESH)

    loads = [
        (value_tab_hbm, table.at[:, 0:48, :]),
        (cell_sel_hbm, cell_sel),
        (spread_hbm, spread),
        (agg_hbm, agg),
        (qkv_hbm.at[0], qkv_w.at[0]),
        (proj_hbm, proj_w),
        (up_hbm, up_w),
        (down_hbm, down_w),
        (quad_sel_hbm, quad_sel),
        (qkv_hbm.at[1], qkv_w.at[1]),
        (quad_back_hbm, quad_back),
        (decode_hbm, decode_w),
    ]
    loads = [pltpu.make_async_copy(a, b, load_sem.at[i]) for i, (a, b) in enumerate(loads)]
    for load in loads:
        load.start()
    (
        got_table,
        got_cells,
        got_spread,
        got_agg,
        got_qkv0,
        got_proj,
        got_up,
        got_down,
        got_quad,
        got_qkv1,
        got_back,
        got_decode,
    ) = loads

    band_sel = band_sel_ref[...]
    gap = jnp.zeros((16, GROUPS * ROWS), BF16)
    for col in range(COLS):
        parts = []
        for lev in range(LEV):
            parts += [fields_ref[v, lev, col] for v in range(LOCAL_VARS)] + [gap]
        turned = dot_t(band_sel, jnp.concatenate(parts, axis=0))
        outgoing[:, col] = turned.reshape(GROUPS, 8, 128).astype(BF16)

    pl.semaphore_wait(barrier, len(peers))

    sends = []
    for k in range(1, GROUPS):
        to = lax.rem(band + k, GROUPS)
        copy = pltpu.make_async_remote_copy(
            src_ref=outgoing.at[to],
            dst_ref=incoming.at[band],
            send_sem=send_sem.at[k],
            recv_sem=recv_sem.at[band],
            device_id=device(to, lon),
            device_id_type=MESH,
        )
        copy.start()
        sends.append(copy)
    own = pltpu.make_async_copy(outgoing.at[band], incoming.at[band], send_sem.at[0])
    own.start()

    row_var = (
        3 * lax.broadcasted_iota(jnp.int32, (GROUPS, 4, PATCH, 128), 0)
        + lax.broadcasted_iota(jnp.int32, (GROUPS, 4, PATCH, 128), 1)
    )
    part = lax.broadcasted_iota(jnp.int32, (GROUPS, 4, PATCH, 128), 1)
    lane = lax.broadcasted_iota(jnp.int32, (GROUPS, 4, PATCH, 128), 3)
    match = (row_var == lane) & (part < 3)
    for h in range(HEADS):
        tab = jnp.broadcast_to(
            score_tab_ref[h].astype(F32)[None, None], (GROUPS, 4, PATCH, 128)
        )
        score_w[:, h * 128 : (h + 1) * 128] = (
            jnp.where(match, tab, 0.0).reshape(KDIM, 128).astype(BF16)
        )
    bias = value_bias_ref[...]
    bias_high = bias.astype(BF16)
    bias_low = (bias - bias_high.astype(F32)).astype(BF16)
    rows = dot(high_ref[...], bias_high) + dot(low_ref[...], bias_low)
    table[:, 48:56, :] = rows.reshape(GROUPS, 8, D).astype(BF16)
    table[:, 56:64, :] = jnp.zeros((GROUPS, 8, D), BF16)
    normed_q[:, SENT:QUAD, :] = jnp.zeros((16, QUAD - SENT, D), BF16)

    own.wait()
    for k in range(1, GROUPS):
        source = lax.rem(band + GROUPS - k, GROUPS)
        pltpu.make_async_remote_copy(
            src_ref=outgoing.at[source],
            dst_ref=incoming.at[source],
            send_sem=send_sem.at[k],
            recv_sem=recv_sem.at[source],
            device_id=device(source, lon),
            device_id_type=MESH,
        ).wait_recv()

    got_cells.wait()
    half = COLS * 8
    low_half = lane_low(half)
    for j in range(GROUPS // 2):
        first = incoming[2 * j].astype(F32).reshape(half, 128)
        second = incoming[2 * j + 1].astype(F32).reshape(half, 128)
        at = slice(j * 128, (j + 1) * 128)
        pool_in[0:half, at] = jnp.where(low_half, first, pltpu.roll(second, 64, 1)).astype(BF16)
        pool_in[half : 2 * half, at] = jnp.where(low_half, pltpu.roll(first, 64, 1), second).astype(BF16)
    cells = (dot(cell_sel[...], pool_in[...]) + ones_ref[...]).astype(BF16)

    got_spread.wait()
    got_table.wait()
    lane128 = lax.broadcasted_iota(jnp.int32, (CELLS, 128), 1)
    real = lane128 < VARS
    low_cells = lane_low(CELLS)
    all_table = table[...].reshape(KDIM, D)
    for pair in range(HEADS // 2):
        kept = None
        for side in range(2):
            h = 2 * pair + side
            at = slice(h * 128, (h + 1) * 128)
            scores = dot(cells, score_w[:, at]) + score_bias_ref[h : h + 1, :]
            scores = jnp.where(real, scores, -jnp.inf)
            top = jnp.max(scores, axis=-1, keepdims=True)
            weights = jnp.exp(scores - top).astype(BF16)
            total = jnp.sum(weights.astype(F32), axis=-1, keepdims=True)
            spread_w = dot(weights, spread[...]).astype(BF16)
            sums = dot(cells * spread_w, all_table[:, pair * 128 : (pair + 1) * 128])
            mean = sums * (1.0 / total)
            kept = mean if kept is None else jnp.where(low_cells, kept, mean)
        pooled[:, pair * 128 : (pair + 1) * 128] = kept.astype(BF16)

    got_agg.wait()
    latent = dot(pooled[...], agg[...])

    normed = layer_norm(latent, gains_ref[0:1, :]).astype(BF16)
    got_qkv0.wait()
    qkv = dot(normed, qkv_w[0]).astype(BF16)
    for pair in range(HEADS // 2):
        at = pair * 128
        context[0:CELLS, at : at + 128] = attention_pair(
            qkv[:, at : at + 128],
            qkv[:, D + at : D + at + 128],
            qkv[:, 2 * D + at : 2 * D + at + 128],
            None,
        )
    got_proj.wait()
    hidden = latent + dot(context[0:CELLS, :], proj_w[0])

    mixed = layer_norm(hidden, gains_ref[1:2, :]).astype(BF16)
    got_up.wait()
    got_down.wait()
    latent = hidden
    for j in range(FF // D):
        at = slice(j * D, (j + 1) * D)
        active = jax.nn.gelu(dot(mixed, up_w[:, at]), approximate=True).astype(BF16)
        latent = latent + dot(active, down_w[at, :])

    normed = layer_norm(latent, gains_ref[2:3, :]).astype(BF16)
    got_quad.wait()
    quads = dot(quad_sel[...], normed).astype(BF16)
    halo = []
    for quad in range(4):
        normed_q[4 * quad] = quads[quad * QUAD : (quad + 1) * QUAD]
        row_half, col_half = quad // 2, quad % 2
        to_band = up_band if row_half == 0 else down_band
        to_lon = left if col_half == 0 else right
        targets = [
            (device(to_band, to_lon), (1 - row_half) * 2 + 1 - col_half, 3),
            (device(to_band, lon), (1 - row_half) * 2 + col_half, 2),
            (device(band, to_lon), row_half * 2 + 1 - col_half, 1),
        ]
        for target, window, slot in targets:
            copy = pltpu.make_async_remote_copy(
                src_ref=normed_q.at[4 * quad, 0:SENT],
                dst_ref=normed_q.at[4 * window + slot, 0:SENT],
                send_sem=halo_send.at[3 * quad + slot - 1],
                recv_sem=halo_recv.at[3 * window + slot - 1],
                device_id=target,
                device_id_type=MESH,
            )
            copy.start()
            halo.append(copy)

    got_qkv1.wait()
    queries = dot(quads, qkv_w[1, :, 0:D]).astype(BF16)
    row_lev = lax.broadcasted_iota(jnp.int32, (QUAD, 4 * QUAD), 0) % 2
    key = lax.broadcasted_iota(jnp.int32, (QUAD, 4 * QUAD), 1)
    place = key % QUAD
    same = (row_lev == place % 2) & (place < QUAD_CELLS)
    near = key < 2 * QUAD
    got_back.wait()

    for copy in halo:
        copy.wait_recv()
    kv2[...] = dot(normed_q[...].reshape(16 * QUAD, D), qkv_w[1, :, D : 3 * D]).astype(BF16)
    for quad in range(4):
        edge = band == (0 if quad // 2 == 0 else GROUPS - 1)
        allowed = same & (near | jnp.logical_not(edge))
        mine = slice(quad * QUAD, (quad + 1) * QUAD)
        keys = slice(quad * 4 * QUAD, (quad + 1) * 4 * QUAD)
        for pair in range(HEADS // 2):
            at = pair * 128
            context[mine, at : at + 128] = attention_pair(
                queries[mine, at : at + 128],
                kv2[keys, at : at + 128],
                kv2[keys, D + at : D + at + 128],
                allowed,
            )
    back = dot(quad_back[...], context[...]).astype(BF16)
    latent = latent + dot(back, proj_w[1])
    final = layer_norm(latent, gains_ref[3:4, :]).astype(BF16)
    got_decode.wait()
    out_ref[...] = (dot(final, decode_w[...]) + decode_bias_ref[...]).astype(BF16)

    for copy in sends:
        copy.wait_send()
    for copy in halo:
        copy.wait_send()


def per_device(
    fields,
    score_table,
    score_bias,
    value_table,
    value_bias,
    agg_weight,
    qkv_weight,
    proj_weight,
    up_weight,
    down_weight,
    norm_gains,
    decode_weight,
    decode_bias,
):
    high, low = bias_rows()
    quads = quad_selector()
    ones = np.zeros((1, KDIM), np.float32)
    for group in range(GROUPS):
        ones[0, group * SLOT + 48 : group * SLOT + 54] = 1
    scores = jnp.pad(score_table.transpose(2, 1, 0), ((0, 0), (0, 0), (0, 128 - VARS)))
    offsets = jnp.pad(score_bias.T, ((0, 0), (0, 128 - VARS)))
    near = [
        fields.transpose(0, 1, 3, 4, 2),
        jnp.asarray(band_selector(), BF16),
        scores,
        offsets,
        value_bias,
        norm_gains,
        decode_bias.reshape(1, -1),
        jnp.asarray(high, BF16),
        jnp.asarray(low, BF16),
        jnp.asarray(ones, F32),
    ]
    far = [
        jnp.asarray(cell_selector(), BF16),
        jnp.asarray(quads, BF16),
        jnp.asarray(quads.T, BF16),
        jnp.asarray(weight_spread(), BF16),
        value_table.reshape(GROUPS, LOCAL_VARS * PATCH, D),
        agg_weight,
        qkv_weight,
        proj_weight,
        up_weight,
        down_weight,
        decode_weight,
    ]
    vmem = pl.BlockSpec(memory_space=pltpu.VMEM)
    hbm = pl.BlockSpec(memory_space=pl.ANY)
    out = pl.pallas_call(
        body,
        out_shape=jax.ShapeDtypeStruct((CELLS, VARS * PATCH), BF16),
        in_specs=[vmem] * len(near) + [hbm] * len(far),
        out_specs=vmem,
        scratch_shapes=[
            pltpu.VMEM((GROUPS, COLS, 8, 128), BF16),
            pltpu.VMEM((GROUPS, COLS, 8, 128), BF16),
            pltpu.VMEM((CELLS, LEV * COLS * 8), BF16),
            pltpu.VMEM((4 * QUAD, CELLS), BF16),
            pltpu.VMEM((CELLS, 4 * QUAD), BF16),
            pltpu.VMEM((128, KDIM), BF16),
            pltpu.VMEM((GROUPS, SLOT, D), BF16),
            pltpu.VMEM((D, D), BF16),
            pltpu.VMEM((2, D, 3 * D), BF16),
            pltpu.VMEM((2, D, D), BF16),
            pltpu.VMEM((D, FF), BF16),
            pltpu.VMEM((FF, D), BF16),
            pltpu.VMEM((D, VARS * PATCH), BF16),
            pltpu.VMEM((KDIM, HEADS * 128), BF16),
            pltpu.VMEM((LEV * COLS * 8, KDIM), BF16),
            pltpu.VMEM((CELLS, D), BF16),
            pltpu.VMEM((16, QUAD, D), BF16),
            pltpu.VMEM((16 * QUAD, 2 * D), BF16),
            pltpu.VMEM((4 * QUAD, D), BF16),
            pltpu.SemaphoreType.DMA((GROUPS,)),
            pltpu.SemaphoreType.DMA((GROUPS,)),
            pltpu.SemaphoreType.DMA((12,)),
            pltpu.SemaphoreType.DMA((12,)),
            pltpu.SemaphoreType.DMA((12,)),
        ],
        compiler_params=pltpu.CompilerParams(
            collective_id=0, has_side_effects=True, vmem_limit_bytes=56 * 1024 * 1024
        ),
        name="forecast_step",
    )(*near, *far)
    return out.reshape(ROWS, COLS, LEV, VARS * PATCH).transpose(2, 0, 1, 3)


def solution(mesh):
    return jax.shard_map(
        per_device,
        mesh=mesh,
        in_specs=(P(("var", "lat"), None, None, "lon", None),) + (P(),) * 12,
        out_specs=P(None, ("var", "lat"), "lon", None),
        check_vma=False,
    )
```

```python
import functools

import jax
import jax.numpy as jnp
import numpy as np
from jax import lax
from jax.experimental import pallas as pl
from jax.experimental.pallas import tpu as pltpu
from jax.sharding import PartitionSpec as P

MESH = pl.DeviceIdType.MESH
EPSILON = 1e-05
F32 = jnp.float32
BF16 = jnp.bfloat16

GROUPS = 16
LONS = 16
LEV, ROWS, COLS = 2, 6, 12
CELLS = LEV * ROWS * COLS
LOCAL_VARS, PATCH, HEADS, HEAD_DIM = 3, 16, 8, 64
VARS = GROUPS * LOCAL_VARS
OWN = LOCAL_VARS * PATCH
D, FF = 512, 2048
PIECES = 18
WIDE = PIECES * OWN
SENT_LANES = 896
SLOT = 64
KDIM = GROUPS * SLOT
QUAD = 48
QUAD_CELLS = 36
SENT = 40


def cell_index(row, col, lev):
    return (row * COLS + col) * LEV + lev


def band_selector():
    out = np.zeros((GROUPS * 8, 4 * 128), np.float32)
    for band in range(GROUPS):
        for row in range(ROWS):
            out[band * 8 + row, band * ROWS + row] = 1
        for j in range(3):
            out[band * 8 + 6, 128 * (1 + j) + band * ROWS + j] = 1
            out[band * 8 + 7, 128 * (1 + j) + band * ROWS + 3 + j] = 1
    return out


def cell_selector():
    out = np.zeros((CELLS, CELLS), np.float32)
    for piece in range(PIECES):
        for k in range(8):
            if k < 6:
                pair, row = piece, k
            else:
                pair, row = PIECES + piece % 6, 3 * (k - 6) + piece // 6
            out[cell_index(row, pair % COLS, pair // COLS), piece * 8 + k] = 1
    return out


def quad_selector():
    out = np.zeros((4 * QUAD, CELLS), np.float32)
    for row in range(ROWS):
        for col in range(COLS):
            for lev in range(LEV):
                quad = (row // 3) * 2 + col // 6
                place = ((row % 3) * 6 + col % 6) * LEV + lev
                out[quad * QUAD + place, cell_index(row, col, lev)] = 1
    return out


def weight_spread():
    out = np.zeros((128, KDIM), np.float32)
    for group in range(GROUPS):
        for var in range(LOCAL_VARS):
            v, at = group * LOCAL_VARS + var, group * SLOT
            out[v, at + var * PATCH : at + (var + 1) * PATCH] = 1
            out[v, at + 48 + var] = 1
            out[v, at + 51 + var] = 1
    return out


def dot(a, b):
    return jnp.dot(a, b, preferred_element_type=F32)


def dot_t(a, b):
    return lax.dot_general(a, b, (((1,), (1,)), ((), ())), preferred_element_type=F32)


def iota(shape, dim):
    return lax.broadcasted_iota(jnp.int32, shape, dim)


def layer_norm(values, gain):
    shifted = values - jnp.mean(values, axis=-1, keepdims=True)
    spread = jnp.mean(shifted * shifted, axis=-1, keepdims=True)
    return shifted * lax.rsqrt(spread + EPSILON) * gain


def own_lanes(stacked, rows):
    head = iota((rows, 256), 1) // HEAD_DIM
    out = stacked[0:rows]
    for a in range(1, 4):
        out = jnp.where(head == a, stacked[a * rows : (a + 1) * rows], out)
    return out


def attention_four(q, k, v, allowed):
    rows = q.shape[0]
    head = iota((rows, 256), 1) // HEAD_DIM
    scaled = q * jnp.asarray(0.125, BF16)
    none = jnp.zeros_like(scaled)
    stacked = jnp.concatenate([jnp.where(head == a, scaled, none) for a in range(4)], axis=0)
    scores = dot_t(stacked, k)
    probs = []
    for a in range(4):
        part = scores[a * rows : (a + 1) * rows]
        if allowed is not None:
            part = jnp.where(allowed, part, -jnp.inf)
        raised = jnp.exp(part - jnp.max(part, axis=-1, keepdims=True))
        probs.append((raised * (1.0 / jnp.sum(raised, axis=-1, keepdims=True))).astype(BF16))
    return own_lanes(dot(jnp.concatenate(probs, axis=0), v), rows).astype(BF16)


def body(
    fields_hbm,
    band_sel_hbm,
    score_tab_hbm,
    score_bias_hbm,
    value_bias_hbm,
    value_tab_hbm,
    spread_hbm,
    cell_sel_hbm,
    agg_hbm,
    gains_hbm,
    qkv_hbm,
    proj_hbm,
    up_hbm,
    down_hbm,
    quad_sel_hbm,
    quad_back_hbm,
    decode_hbm,
    decode_bias_hbm,
    out_ref,
    fields,
    band_sel,
    score_tab,
    score_bias,
    value_bias,
    table,
    spread,
    cell_sel,
    agg,
    gains,
    qkv_w,
    proj_w,
    up_w,
    down_w,
    quad_sel,
    quad_back,
    decode_w,
    decode_bias,
    lifted,
    outgoing,
    incoming,
    score_wide,
    score_w,
    bias_wide,
    raw,
    weights_all,
    quads,
    window,
    context,
    returned,
    send_sem,
    recv_sem,
    halo_send,
    halo_recv,
    load_sem,
):
    var, lon, lat = lax.axis_index("var"), lax.axis_index("lon"), lax.axis_index("lat")
    band = var * 2 + lat
    up_band, down_band = lax.rem(band + GROUPS - 1, GROUPS), lax.rem(band + 1, GROUPS)
    left, right = lax.rem(lon + LONS - 1, LONS), lax.rem(lon + 1, LONS)

    def device(of_band, of_lon):
        return (of_band // 2, of_lon, lax.rem(of_band, 2))

    loads = {
        "fields": (fields_hbm, fields),
        "band_sel": (band_sel_hbm, band_sel),
        "score_tab": (score_tab_hbm, score_tab),
        "score_bias": (score_bias_hbm, score_bias),
        "value_bias": (value_bias_hbm, value_bias),
        "table": (value_tab_hbm, table.at[:, 0:OWN, :]),
        "spread": (spread_hbm, spread),
        "cell_sel": (cell_sel_hbm, cell_sel),
        "agg": (agg_hbm, agg),
        "gains": (gains_hbm, gains),
        "qkv0": (qkv_hbm.at[0], qkv_w.at[0]),
        "proj": (proj_hbm, proj_w),
        "up": (up_hbm, up_w),
        "down": (down_hbm, down_w),
        "quad_sel": (quad_sel_hbm, quad_sel),
        "qkv1": (qkv_hbm.at[1], qkv_w.at[1]),
        "quad_back": (quad_back_hbm, quad_back),
        "decode": (decode_hbm, decode_w),
        "decode_bias": (decode_bias_hbm, decode_bias),
    }
    loads = {
        name: pltpu.make_async_copy(a, b, load_sem.at[i]) for i, (name, (a, b)) in enumerate(loads.items())
    }
    loads["fields"].start()
    loads["band_sel"].start()

    barrier = pltpu.get_barrier_semaphore()
    peers = [device(lax.rem(band + k, GROUPS), lon) for k in range(1, GROUPS)]
    peers += [device(up_band, left), device(band, left), device(down_band, right), device(band, right)]
    for peer in peers:
        pl.semaphore_signal(barrier, inc=1, device_id=peer, device_id_type=MESH)

    lifted[...] = jnp.zeros(lifted.shape, BF16)
    loads["fields"].wait()
    loads["band_sel"].wait()
    rows = GROUPS * ROWS
    half = COLS // 2
    for v in range(LOCAL_VARS):
        lifted[0:COLS, v, :, 0:rows] = fields[v, 0]
        lifted[COLS:PIECES, v, :, 0:rows] = fields[v, 1, 0:half]
        for j in range(3):
            lifted[6 * j : 6 * j + 6, v, :, 128 * (1 + j) : 128 * (1 + j) + rows] = fields[v, 1, half:COLS]
    turned = dot_t(band_sel[...], lifted[...].reshape(WIDE, 512))
    outgoing[:, :, 0:WIDE] = turned.reshape(GROUPS, 8, WIDE).astype(BF16)

    pl.semaphore_wait(barrier, len(peers))

    sends = []
    for k in range(1, GROUPS):
        to = lax.rem(band + k, GROUPS)
        copy = pltpu.make_async_remote_copy(
            src_ref=outgoing.at[to],
            dst_ref=incoming.at[band],
            send_sem=send_sem.at[k],
            recv_sem=recv_sem.at[band],
            device_id=device(to, lon),
            device_id_type=MESH,
        )
        copy.start()
        sends.append(copy)
    own = pltpu.make_async_copy(outgoing.at[band], incoming.at[band], send_sem.at[0])
    own.start()
    for name, load in loads.items():
        if name not in ("fields", "band_sel"):
            load.start()

    shape = (GROUPS, 4, PATCH, 128)
    part = iota(shape, 1)
    match = (3 * iota(shape, 0) + part == iota(shape, 3)) & (part < 3)
    score_wide[...] = jnp.zeros(score_wide.shape, F32)
    bias_wide[...] = jnp.zeros(bias_wide.shape, F32)
    loads["score_tab"].wait()
    score_wide[:, :, 0:VARS] = score_tab[...].astype(F32)
    for h in range(HEADS):
        tab = jnp.broadcast_to(score_wide[:, h, :][None, None], shape)
        score_w[:, h * 128 : (h + 1) * 128] = jnp.where(match, tab, 0.0).reshape(KDIM, 128).astype(BF16)
    loads["score_bias"].wait()
    bias_wide[:, 0:VARS] = score_bias[...]
    loads["value_bias"].wait()
    bias = value_bias[...]
    bias_high = bias.astype(BF16)
    bias_low = (bias - bias_high.astype(F32)).astype(BF16)
    at_row, at_var = iota((GROUPS * 8, VARS), 0), iota((GROUPS * 8, VARS), 1)
    kind, first = at_row % 8, 3 * (at_row // 8)
    high = jnp.where((kind < 3) & (at_var == first + kind), 1.0, 0.0).astype(BF16)
    low = jnp.where((kind > 2) & (kind < 6) & (at_var == first + kind - 3), 1.0, 0.0).astype(BF16)
    bias_rows = dot(high, bias_high) + dot(low, bias_low)
    table[:, OWN : OWN + 8, :] = bias_rows.reshape(GROUPS, 8, D).astype(BF16)
    table[:, OWN + 8 : SLOT, :] = jnp.zeros((GROUPS, 8, D), BF16)
    window[:, SENT:QUAD, :] = jnp.zeros((4, QUAD - SENT, D), BF16)
    returned[:, SENT:QUAD, :] = jnp.zeros((4, QUAD - SENT, D), BF16)
    for name in ("table", "spread", "cell_sel"):
        loads[name].wait()

    own.wait()
    for k in range(1, GROUPS):
        source = lax.rem(band + GROUPS - k, GROUPS)
        pltpu.make_async_remote_copy(
            src_ref=outgoing.at[source],
            dst_ref=incoming.at[source],
            send_sem=send_sem.at[k],
            recv_sem=recv_sem.at[source],
            device_id=device(source, lon),
            device_id_type=MESH,
        ).wait_recv()

    lane = iota((8, 128), 1)
    in_first = lane < OWN
    in_second = (lane >= SLOT) & (lane < SLOT + OWN)
    ones = jnp.where((lane % SLOT >= OWN) & (lane % SLOT < OWN + 6), 1.0, 0.0)
    for j in range(GROUPS // 2):
        two = [incoming[2 * j].astype(F32), incoming[2 * j + 1].astype(F32)]
        for piece in range(PIECES):
            tile, at = divmod(piece * OWN, 128)
            moved = []
            for side in range(2):
                x = two[side][:, tile * 128 : (tile + 1) * 128]
                if at + OWN > 128:
                    x = jnp.where(lane >= at, x, two[side][:, (tile + 1) * 128 : (tile + 2) * 128])
                shift = (SLOT * side - at) % 128
                moved.append(pltpu.roll(x, shift, 1) if shift else x)
            raw[8 * piece : 8 * piece + 8, j * 128 : (j + 1) * 128] = jnp.where(
                in_first, moved[0], jnp.where(in_second, moved[1], ones)
            )
    cells = raw[...].astype(BF16)

    real = iota((CELLS, 128), 1) < VARS
    totals = []
    for h in range(HEADS):
        scores = dot(cells, score_w[:, h * 128 : (h + 1) * 128]) + bias_wide[h : h + 1, :]
        scores = jnp.where(real, scores, -jnp.inf)
        weights = jnp.exp(scores - jnp.max(scores, axis=-1, keepdims=True)).astype(BF16)
        totals.append(1.0 / jnp.sum(weights.astype(F32), axis=-1, keepdims=True))
        weights_all[h * CELLS : (h + 1) * CELLS, :] = weights
    all_table = table[...].reshape(KDIM, D)
    groups = []
    for g in range(2):
        own_weights = weights_all[4 * g * CELLS : 4 * (g + 1) * CELLS, :]
        sums = None
        for t in range(KDIM // 256):
            at = slice(t * 256, (t + 1) * 256)
            spread_w = dot(own_weights, spread[:, at]).astype(BF16)
            repeated = jnp.concatenate([cells[:, at]] * 4, axis=0)
            more = dot(repeated * spread_w, all_table[at, g * 256 : (g + 1) * 256])
            sums = more if sums is None else sums + more
        scaled = [sums[a * CELLS : (a + 1) * CELLS] * totals[4 * g + a] for a in range(4)]
        groups.append(own_lanes(jnp.concatenate(scaled, axis=0), CELLS).astype(BF16))
    pooled = jnp.concatenate(groups, axis=1)
    pooled = dot(cell_sel[...], pooled).astype(BF16)

    loads["agg"].wait()
    latent = dot(pooled, agg[...])

    loads["gains"].wait()
    normed = layer_norm(latent, gains[0:1, :]).astype(BF16)
    loads["qkv0"].wait()
    qkv = dot(normed, qkv_w[0]).astype(BF16)
    mixed = jnp.concatenate(
        [
            attention_four(
                qkv[:, at : at + 256], qkv[:, D + at : D + at + 256], qkv[:, 2 * D + at : 2 * D + at + 256], None
            )
            for at in (0, 256)
        ],
        axis=1,
    )
    loads["proj"].wait()
    hidden = latent + dot(mixed, proj_w[0])

    mixed = layer_norm(hidden, gains[1:2, :]).astype(BF16)
    loads["up"].wait()
    loads["down"].wait()
    latent = hidden
    for j in range(FF // D):
        at = slice(j * D, (j + 1) * D)
        active = jax.nn.gelu(dot(mixed, up_w[:, at]), approximate=True).astype(BF16)
        latent = latent + dot(active, down_w[at, :])

    normed = layer_norm(latent, gains[2:3, :]).astype(BF16)
    loads["quad_sel"].wait()
    quarters = dot(quad_sel[...], normed).astype(BF16).reshape(4, QUAD, D)
    quads[...] = quarters
    window[0] = quarters[3]
    owners = [device(up_band, left), device(up_band, lon), device(band, left)]
    users = [device(down_band, right), device(down_band, lon), device(band, right)]
    out_copies = []
    for quad in range(3):
        copy = pltpu.make_async_remote_copy(
            src_ref=quads.at[quad, 0:SENT],
            dst_ref=window.at[3 - quad, 0:SENT],
            send_sem=halo_send.at[quad],
            recv_sem=halo_recv.at[quad],
            device_id=owners[quad],
            device_id_type=MESH,
        )
        copy.start()
        out_copies.append(copy)

    at_query, at_key = iota((4 * QUAD, 4 * QUAD), 0), iota((4 * QUAD, 4 * QUAD), 1)
    allowed = (at_query % 2 == at_key % 2) & (at_key % QUAD < QUAD_CELLS)
    same_half = (at_query < 2 * QUAD) == (at_key < 2 * QUAD)
    allowed = allowed & (same_half | (band != GROUPS - 1))
    for name in ("qkv1", "quad_back", "decode", "decode_bias"):
        loads[name].wait()
    for copy in out_copies:
        copy.wait_recv()
    qkv = dot(window[...].reshape(4 * QUAD, D), qkv_w[1]).astype(BF16)
    for at in (0, 256):
        context[:, :, at : at + 256] = attention_four(
            qkv[:, at : at + 256], qkv[:, D + at : D + at + 256], qkv[:, 2 * D + at : 2 * D + at + 256], allowed
        ).reshape(4, QUAD, 256)
    returned[3] = context[0]
    back_copies = []
    for quad in range(3):
        copy = pltpu.make_async_remote_copy(
            src_ref=context.at[3 - quad, 0:SENT],
            dst_ref=returned.at[quad, 0:SENT],
            send_sem=halo_send.at[3 + quad],
            recv_sem=halo_recv.at[3 + quad],
            device_id=users[quad],
            device_id_type=MESH,
        )
        copy.start()
        back_copies.append(copy)
    for copy in back_copies:
        copy.wait_recv()
    mixed = dot(quad_back[...], returned[...].reshape(4 * QUAD, D)).astype(BF16)
    latent = latent + dot(mixed, proj_w[1])
    final = layer_norm(latent, gains[3:4, :]).astype(BF16)
    offsets = jnp.concatenate([decode_bias[i : i + 1, :] for i in range(VARS * PATCH // 128)], axis=1)
    out_ref[...] = (dot(final, decode_w[...]) + offsets).astype(BF16)

    for copy in sends + out_copies + back_copies:
        copy.wait_send()


def per_device(
    fields,
    score_table,
    score_bias,
    value_table,
    value_bias,
    agg_weight,
    qkv_weight,
    proj_weight,
    up_weight,
    down_weight,
    norm_gains,
    decode_weight,
    decode_bias,
):
    quads = quad_selector()
    operands = [
        fields.transpose(0, 1, 3, 4, 2),
        jnp.asarray(band_selector(), BF16),
        score_table.transpose(1, 2, 0),
        score_bias.T,
        value_bias,
        value_table.reshape(GROUPS, OWN, D),
        jnp.asarray(weight_spread(), BF16),
        jnp.asarray(cell_selector(), BF16),
        agg_weight,
        norm_gains,
        qkv_weight,
        proj_weight,
        up_weight,
        down_weight,
        jnp.asarray(quads, BF16),
        jnp.asarray(quads.T, BF16),
        decode_weight,
        decode_bias.reshape(-1, 128),
    ]
    own = [jax.ShapeDtypeStruct(x.shape, x.dtype) for x in operands]
    own[5] = jax.ShapeDtypeStruct((GROUPS, SLOT, D), BF16)
    out = pl.pallas_call(
        body,
        out_shape=jax.ShapeDtypeStruct((CELLS, VARS * PATCH), BF16),
        in_specs=[pl.BlockSpec(memory_space=pl.ANY)] * len(operands),
        out_specs=pl.BlockSpec(memory_space=pltpu.VMEM),
        scratch_shapes=[pltpu.VMEM(x.shape, x.dtype) for x in own]
        + [
            pltpu.VMEM((PIECES, LOCAL_VARS, PATCH, 512), BF16),
            pltpu.VMEM((GROUPS, 8, SENT_LANES), BF16),
            pltpu.VMEM((GROUPS, 8, SENT_LANES), BF16),
            pltpu.VMEM((PATCH, HEADS, 128), F32),
            pltpu.VMEM((KDIM, HEADS * 128), BF16),
            pltpu.VMEM((HEADS, 128), F32),
            pltpu.VMEM((CELLS, KDIM), F32),
            pltpu.VMEM((HEADS * CELLS, 128), BF16),
            pltpu.VMEM((4, QUAD, D), BF16),
            pltpu.VMEM((4, QUAD, D), BF16),
            pltpu.VMEM((4, QUAD, D), BF16),
            pltpu.VMEM((4, QUAD, D), BF16),
            pltpu.SemaphoreType.DMA((GROUPS,)),
            pltpu.SemaphoreType.DMA((GROUPS,)),
            pltpu.SemaphoreType.DMA((6,)),
            pltpu.SemaphoreType.DMA((6,)),
            pltpu.SemaphoreType.DMA((len(operands) + 1,)),
        ],
        compiler_params=pltpu.CompilerParams(
            collective_id=0, has_side_effects=True, vmem_limit_bytes=56 * 1024 * 1024
        ),
        name="forecast_step",
    )(*operands)
    return out.reshape(ROWS, COLS, LEV, VARS * PATCH).transpose(2, 0, 1, 3)


def solution(mesh):
    return jax.shard_map(
        per_device,
        mesh=mesh,
        in_specs=(P(("var", "lat"), None, None, "lon", None),) + (P(),) * 12,
        out_specs=P(None, ("var", "lat"), "lon", None),
        check_vma=False,
    )
```

```python
import functools

import jax
import jax.numpy as jnp
import numpy as np
from jax import lax
from jax.experimental import pallas as pl
from jax.experimental.pallas import tpu as pltpu
from jax.sharding import PartitionSpec as P

MESH = pl.DeviceIdType.MESH
EPSILON = 1e-05
F32 = jnp.float32
BF16 = jnp.bfloat16

GROUPS = 16
LONS = 16
LEV, ROWS, COLS = 2, 6, 12
CELLS = LEV * ROWS * COLS
LOCAL_VARS, PATCH, HEADS, HEAD_DIM = 3, 16, 8, 64
VARS = GROUPS * LOCAL_VARS
OWN = LOCAL_VARS * PATCH
D, FF = 512, 2048
PIECES = 18
WIDE = PIECES * OWN
SENT_LANES = 896
SLOT = 64
KDIM = GROUPS * SLOT
QUAD = 48
QUAD_CELLS = 36
SENT = 40


def cell_index(row, col, lev):
    return (row * COLS + col) * LEV + lev


def band_selector():
    out = np.zeros((GROUPS * 8, 4 * 128), np.float32)
    for band in range(GROUPS):
        for row in range(ROWS):
            out[band * 8 + row, band * ROWS + row] = 1
        for j in range(3):
            out[band * 8 + 6, 128 * (1 + j) + band * ROWS + j] = 1
            out[band * 8 + 7, 128 * (1 + j) + band * ROWS + 3 + j] = 1
    return out


def cell_selector():
    out = np.zeros((CELLS, CELLS), np.float32)
    for piece in range(PIECES):
        for k in range(8):
            if k < 6:
                pair, row = piece, k
            else:
                pair, row = PIECES + piece % 6, 3 * (k - 6) + piece // 6
            out[cell_index(row, pair % COLS, pair // COLS), piece * 8 + k] = 1
    return out


def quad_selector():
    out = np.zeros((4 * QUAD, CELLS), np.float32)
    for row in range(ROWS):
        for col in range(COLS):
            for lev in range(LEV):
                quad = (row // 3) * 2 + col // 6
                place = ((row % 3) * 6 + col % 6) * LEV + lev
                out[quad * QUAD + place, cell_index(row, col, lev)] = 1
    return out


def weight_spread():
    out = np.zeros((128, KDIM), np.float32)
    for group in range(GROUPS):
        for var in range(LOCAL_VARS):
            v, at = group * LOCAL_VARS + var, group * SLOT
            out[v, at + var * PATCH : at + (var + 1) * PATCH] = 1
            out[v, at + 48 + var] = 1
            out[v, at + 51 + var] = 1
    return out


def dot(a, b):
    return jnp.dot(a, b, preferred_element_type=F32)


def dot_t(a, b):
    return lax.dot_general(a, b, (((1,), (1,)), ((), ())), preferred_element_type=F32)


def iota(shape, dim):
    return lax.broadcasted_iota(jnp.int32, shape, dim)


def layer_norm(values, gain):
    shifted = values - jnp.mean(values, axis=-1, keepdims=True)
    spread = jnp.mean(shifted * shifted, axis=-1, keepdims=True)
    return shifted * lax.rsqrt(spread + EPSILON) * gain


def own_lanes(stacked, rows):
    head = iota((rows, 256), 1) // HEAD_DIM
    out = stacked[0:rows]
    for a in range(1, 4):
        out = jnp.where(head == a, stacked[a * rows : (a + 1) * rows], out)
    return out


def attention_four(q, k, v, allowed):
    rows = q.shape[0]
    head = iota((rows, 256), 1) // HEAD_DIM
    scaled = q * jnp.asarray(0.125, BF16)
    none = jnp.zeros_like(scaled)
    stacked = jnp.concatenate([jnp.where(head == a, scaled, none) for a in range(4)], axis=0)
    scores = dot_t(stacked, k)
    probs = []
    for a in range(4):
        part = scores[a * rows : (a + 1) * rows]
        if allowed is not None:
            part = jnp.where(allowed, part, -jnp.inf)
        raised = jnp.exp(part - jnp.max(part, axis=-1, keepdims=True))
        probs.append((raised * (1.0 / jnp.sum(raised, axis=-1, keepdims=True))).astype(BF16))
    return own_lanes(dot(jnp.concatenate(probs, axis=0), v), rows).astype(BF16)


def body(
    fields_hbm,
    band_sel_hbm,
    score_tab_hbm,
    score_bias_hbm,
    value_bias_hbm,
    value_tab_hbm,
    spread_hbm,
    cell_sel_hbm,
    agg_hbm,
    gains_hbm,
    qkv_hbm,
    proj_hbm,
    up_hbm,
    down_hbm,
    quad_sel_hbm,
    quad_back_hbm,
    decode_hbm,
    decode_bias_hbm,
    out_ref,
    fields,
    band_sel,
    score_tab,
    score_bias,
    value_bias,
    table,
    spread,
    cell_sel,
    agg,
    gains,
    qkv_w,
    proj_w,
    up_w,
    down_w,
    quad_sel,
    quad_back,
    decode_w,
    decode_bias,
    lifted,
    outgoing,
    incoming,
    score_wide,
    score_w,
    bias_wide,
    raw,
    weights_all,
    quads,
    window,
    context,
    returned,
    edge,
    edge_context,
    send_sem,
    recv_sem,
    halo_send,
    halo_recv,
    load_sem,
):
    var, lon, lat = lax.axis_index("var"), lax.axis_index("lon"), lax.axis_index("lat")
    band = var * 2 + lat
    up_band, down_band = lax.rem(band + GROUPS - 1, GROUPS), lax.rem(band + 1, GROUPS)
    left, right = lax.rem(lon + LONS - 1, LONS), lax.rem(lon + 1, LONS)

    def device(of_band, of_lon):
        return (of_band // 2, of_lon, lax.rem(of_band, 2))

    loads = {
        "fields": (fields_hbm, fields),
        "band_sel": (band_sel_hbm, band_sel),
        "score_tab": (score_tab_hbm, score_tab),
        "score_bias": (score_bias_hbm, score_bias),
        "value_bias": (value_bias_hbm, value_bias),
        "table": (value_tab_hbm, table.at[:, 0:OWN, :]),
        "spread": (spread_hbm, spread),
        "cell_sel": (cell_sel_hbm, cell_sel),
        "agg": (agg_hbm, agg),
        "gains": (gains_hbm, gains),
        "qkv0": (qkv_hbm.at[0], qkv_w.at[0]),
        "proj": (proj_hbm, proj_w),
        "up": (up_hbm, up_w),
        "down": (down_hbm, down_w),
        "quad_sel": (quad_sel_hbm, quad_sel),
        "qkv1": (qkv_hbm.at[1], qkv_w.at[1]),
        "quad_back": (quad_back_hbm, quad_back),
        "decode": (decode_hbm, decode_w),
        "decode_bias": (decode_bias_hbm, decode_bias),
    }
    loads = {
        name: pltpu.make_async_copy(a, b, load_sem.at[i]) for i, (name, (a, b)) in enumerate(loads.items())
    }
    loads["fields"].start()
    loads["band_sel"].start()

    barrier = pltpu.get_barrier_semaphore()
    peers = [device(lax.rem(band + k, GROUPS), lon) for k in range(1, GROUPS)]
    peers += [device(up_band, left), device(band, left), device(down_band, right), device(band, right)]
    for peer in peers:
        pl.semaphore_signal(barrier, inc=1, device_id=peer, device_id_type=MESH)

    lifted[...] = jnp.zeros(lifted.shape, BF16)
    loads["fields"].wait()
    loads["band_sel"].wait()
    rows = GROUPS * ROWS
    half = COLS // 2
    for v in range(LOCAL_VARS):
        lifted[0:COLS, v, :, 0:rows] = fields[v, 0]
        lifted[COLS:PIECES, v, :, 0:rows] = fields[v, 1, 0:half]
        for j in range(3):
            lifted[6 * j : 6 * j + 6, v, :, 128 * (1 + j) : 128 * (1 + j) + rows] = fields[v, 1, half:COLS]
    turned = dot_t(band_sel[...], lifted[...].reshape(WIDE, 512))
    outgoing[:, :, 0:WIDE] = turned.reshape(GROUPS, 8, WIDE).astype(BF16)

    pl.semaphore_wait(barrier, len(peers))

    sends = []
    for k in range(1, GROUPS):
        to = lax.rem(band + k, GROUPS)
        copy = pltpu.make_async_remote_copy(
            src_ref=outgoing.at[to],
            dst_ref=incoming.at[band],
            send_sem=send_sem.at[k],
            recv_sem=recv_sem.at[band],
            device_id=device(to, lon),
            device_id_type=MESH,
        )
        copy.start()
        sends.append(copy)
    own = pltpu.make_async_copy(outgoing.at[band], incoming.at[band], send_sem.at[0])
    own.start()
    for name, load in loads.items():
        if name not in ("fields", "band_sel"):
            load.start()

    shape = (GROUPS, 4, PATCH, 128)
    part = iota(shape, 1)
    match = (3 * iota(shape, 0) + part == iota(shape, 3)) & (part < 3)
    score_wide[...] = jnp.zeros(score_wide.shape, F32)
    bias_wide[...] = jnp.zeros(bias_wide.shape, F32)
    loads["score_tab"].wait()
    score_wide[:, :, 0:VARS] = score_tab[...].astype(F32)
    for h in range(HEADS):
        tab = jnp.broadcast_to(score_wide[:, h, :][None, None], shape)
        score_w[:, h * 128 : (h + 1) * 128] = jnp.where(match, tab, 0.0).reshape(KDIM, 128).astype(BF16)
    loads["score_bias"].wait()
    bias_wide[:, 0:VARS] = score_bias[...]
    loads["value_bias"].wait()
    bias = value_bias[...]
    bias_high = bias.astype(BF16)
    bias_low = (bias - bias_high.astype(F32)).astype(BF16)
    at_row, at_var = iota((GROUPS * 8, VARS), 0), iota((GROUPS * 8, VARS), 1)
    kind, first = at_row % 8, 3 * (at_row // 8)
    high = jnp.where((kind < 3) & (at_var == first + kind), 1.0, 0.0).astype(BF16)
    low = jnp.where((kind > 2) & (kind < 6) & (at_var == first + kind - 3), 1.0, 0.0).astype(BF16)
    bias_rows = dot(high, bias_high) + dot(low, bias_low)
    table[:, OWN : OWN + 8, :] = bias_rows.reshape(GROUPS, 8, D).astype(BF16)
    table[:, OWN + 8 : SLOT, :] = jnp.zeros((GROUPS, 8, D), BF16)
    window[:, SENT:QUAD, :] = jnp.zeros((4, QUAD - SENT, D), BF16)
    returned[:, SENT:QUAD, :] = jnp.zeros((4, QUAD - SENT, D), BF16)
    edge[:, SENT:QUAD, :] = jnp.zeros((2, QUAD - SENT, D), BF16)
    first_band, last_band = band == 0, band == GROUPS - 1

    @pl.when(first_band)
    def _():
        window[2:4, 0:SENT, :] = jnp.zeros((2, SENT, D), BF16)

    for name in ("table", "spread", "cell_sel"):
        loads[name].wait()

    own.wait()
    lane = iota((8, 128), 1)
    in_first = lane < OWN
    in_second = (lane >= SLOT) & (lane < SLOT + OWN)
    ones = jnp.where((lane % SLOT >= OWN) & (lane % SLOT < OWN + 6), 1.0, 0.0)
    for j in range(GROUPS // 2):
        for source in (2 * j, 2 * j + 1):
            arrival = pltpu.make_async_remote_copy(
                src_ref=outgoing.at[source],
                dst_ref=incoming.at[source],
                send_sem=send_sem.at[source],
                recv_sem=recv_sem.at[source],
                device_id=device(source, lon),
                device_id_type=MESH,
            )
            pl.when(band != source)(arrival.wait_recv)
        two = [incoming[2 * j].astype(F32), incoming[2 * j + 1].astype(F32)]
        for piece in range(PIECES):
            tile, at = divmod(piece * OWN, 128)
            moved = []
            for side in range(2):
                x = two[side][:, tile * 128 : (tile + 1) * 128]
                if at + OWN > 128:
                    x = jnp.where(lane >= at, x, two[side][:, (tile + 1) * 128 : (tile + 2) * 128])
                shift = (SLOT * side - at) % 128
                moved.append(pltpu.roll(x, shift, 1) if shift else x)
            raw[8 * piece : 8 * piece + 8, j * 128 : (j + 1) * 128] = jnp.where(
                in_first, moved[0], jnp.where(in_second, moved[1], ones)
            )
    cells = raw[...].astype(BF16)

    real = iota((CELLS, 128), 1) < VARS
    totals = []
    for h in range(HEADS):
        scores = dot(cells, score_w[:, h * 128 : (h + 1) * 128]) + bias_wide[h : h + 1, :]
        scores = jnp.where(real, scores, -jnp.inf)
        weights = jnp.exp(scores - jnp.max(scores, axis=-1, keepdims=True)).astype(BF16)
        totals.append(1.0 / jnp.sum(weights.astype(F32), axis=-1, keepdims=True))
        weights_all[h * CELLS : (h + 1) * CELLS, :] = weights
    all_table = table[...].reshape(KDIM, D)
    groups = []
    for g in range(2):
        own_weights = weights_all[4 * g * CELLS : 4 * (g + 1) * CELLS, :]
        sums = None
        for t in range(KDIM // 256):
            at = slice(t * 256, (t + 1) * 256)
            spread_w = dot(own_weights, spread[:, at]).astype(BF16)
            repeated = jnp.concatenate([cells[:, at]] * 4, axis=0)
            more = dot(repeated * spread_w, all_table[at, g * 256 : (g + 1) * 256])
            sums = more if sums is None else sums + more
        scaled = [sums[a * CELLS : (a + 1) * CELLS] * totals[4 * g + a] for a in range(4)]
        groups.append(own_lanes(jnp.concatenate(scaled, axis=0), CELLS).astype(BF16))
    pooled = jnp.concatenate(groups, axis=1)
    pooled = dot(cell_sel[...], pooled).astype(BF16)

    loads["agg"].wait()
    latent = dot(pooled, agg[...])

    loads["gains"].wait()
    normed = layer_norm(latent, gains[0:1, :]).astype(BF16)
    loads["qkv0"].wait()
    qkv = dot(normed, qkv_w[0]).astype(BF16)
    mixed = jnp.concatenate(
        [
            attention_four(
                qkv[:, at : at + 256], qkv[:, D + at : D + at + 256], qkv[:, 2 * D + at : 2 * D + at + 256], None
            )
            for at in (0, 256)
        ],
        axis=1,
    )
    loads["proj"].wait()
    hidden = latent + dot(mixed, proj_w[0])

    mixed = layer_norm(hidden, gains[1:2, :]).astype(BF16)
    loads["up"].wait()
    loads["down"].wait()
    latent = hidden
    for j in range(FF // D):
        at = slice(j * D, (j + 1) * D)
        active = jax.nn.gelu(dot(mixed, up_w[:, at]), approximate=True).astype(BF16)
        latent = latent + dot(active, down_w[at, :])

    normed = layer_norm(latent, gains[2:3, :]).astype(BF16)
    loads["quad_sel"].wait()
    quarters = dot(quad_sel[...], normed).astype(BF16).reshape(4, QUAD, D)
    quads[...] = quarters
    window[0] = quarters[0]

    def halo(source, target, sent, arrived, to):
        return pltpu.make_async_remote_copy(
            src_ref=source,
            dst_ref=target,
            send_sem=halo_send.at[sent],
            recv_sem=halo_recv.at[arrived],
            device_id=to,
            device_id_type=MESH,
        )

    rows = slice(0, SENT)
    out_right = halo(quads.at[1, rows], window.at[1, rows], 0, 0, device(band, right))
    out_down = halo(quads.at[2, rows], window.at[2, rows], 1, 1, device(down_band, lon))
    out_corner = halo(quads.at[3, rows], window.at[3, rows], 2, 2, device(down_band, right))
    out_edge = halo(quads.at[3, rows], edge.at[1, rows], 3, 3, device(band, right))
    back_left = halo(context.at[1, rows], returned.at[1, rows], 4, 4, device(band, left))
    back_up = halo(context.at[2, rows], returned.at[2, rows], 5, 5, device(up_band, lon))
    back_corner = halo(context.at[3, rows], returned.at[3, rows], 6, 6, device(up_band, left))
    back_edge = halo(edge_context.at[1, rows], returned.at[3, rows], 7, 6, device(band, left))

    @pl.when(jnp.logical_not(last_band))
    def _():
        out_corner.start()
        out_down.start()

    out_right.start()

    @pl.when(last_band)
    def _():
        out_edge.start()
        edge[0] = quads[2]

    at_query, at_key = iota((4 * QUAD, 4 * QUAD), 0), iota((4 * QUAD, 4 * QUAD), 1)
    same_level = (at_query % 2 == at_key % 2) & (at_key % QUAD < QUAD_CELLS)
    same_half = (at_query < 2 * QUAD) == (at_key < 2 * QUAD)
    allowed = same_level & (same_half | jnp.logical_not(first_band))
    for name in ("qkv1", "quad_back", "decode", "decode_bias"):
        loads[name].wait()

    def window_context(cells_in, out, mask):
        count = 4 if out is context else 2
        qkv = dot(cells_in[...].reshape(count * QUAD, D), qkv_w[1]).astype(BF16)
        for at in (0, 256):
            out[:, :, at : at + 256] = attention_four(
                qkv[:, at : at + 256], qkv[:, D + at : D + at + 256], qkv[:, 2 * D + at : 2 * D + at + 256], mask
            ).reshape(count, QUAD, 256)

    out_right.wait_recv()

    @pl.when(jnp.logical_not(first_band))
    def _():
        out_down.wait_recv()
        out_corner.wait_recv()

    window_context(window, context, allowed)

    @pl.when(jnp.logical_not(first_band))
    def _():
        back_corner.start()
        back_up.start()

    back_left.start()
    returned[0] = context[0]

    @pl.when(last_band)
    def _():
        out_edge.wait_recv()
        window_context(edge, edge_context, same_level[0 : 2 * QUAD, 0 : 2 * QUAD])
        back_edge.start()
        returned[2] = edge_context[0]

    back_left.wait_recv()
    back_corner.wait_recv()

    @pl.when(jnp.logical_not(last_band))
    def _():
        back_up.wait_recv()

    mixed = dot(quad_back[...], returned[...].reshape(4 * QUAD, D)).astype(BF16)
    latent = latent + dot(mixed, proj_w[1])
    final = layer_norm(latent, gains[3:4, :]).astype(BF16)
    offsets = jnp.concatenate([decode_bias[i : i + 1, :] for i in range(VARS * PATCH // 128)], axis=1)
    out_ref[...] = (dot(final, decode_w[...]) + offsets).astype(BF16).reshape(CELLS // LEV, LEV, VARS * PATCH)

    for copy in sends + [out_right, back_left]:
        copy.wait_send()

    @pl.when(jnp.logical_not(last_band))
    def _():
        out_down.wait_send()
        out_corner.wait_send()

    @pl.when(jnp.logical_not(first_band))
    def _():
        back_up.wait_send()
        back_corner.wait_send()

    @pl.when(last_band)
    def _():
        out_edge.wait_send()
        back_edge.wait_send()


def per_device(
    fields,
    score_table,
    score_bias,
    value_table,
    value_bias,
    agg_weight,
    qkv_weight,
    proj_weight,
    up_weight,
    down_weight,
    norm_gains,
    decode_weight,
    decode_bias,
):
    quads = quad_selector()
    operands = [
        fields.transpose(0, 1, 3, 4, 2),
        jnp.asarray(band_selector(), BF16),
        score_table.transpose(1, 2, 0),
        score_bias.T,
        value_bias,
        value_table.reshape(GROUPS, OWN, D),
        jnp.asarray(weight_spread(), BF16),
        jnp.asarray(cell_selector(), BF16),
        agg_weight,
        norm_gains,
        qkv_weight,
        proj_weight,
        up_weight,
        down_weight,
        jnp.asarray(quads, BF16),
        jnp.asarray(quads.T, BF16),
        decode_weight,
        decode_bias.reshape(-1, 128),
    ]
    own = [jax.ShapeDtypeStruct(x.shape, x.dtype) for x in operands]
    own[5] = jax.ShapeDtypeStruct((GROUPS, SLOT, D), BF16)
    out = pl.pallas_call(
        body,
        out_shape=jax.ShapeDtypeStruct((CELLS // LEV, LEV, VARS * PATCH), BF16),
        in_specs=[pl.BlockSpec(memory_space=pl.ANY)] * len(operands),
        out_specs=pl.BlockSpec(memory_space=pltpu.VMEM),
        scratch_shapes=[pltpu.VMEM(x.shape, x.dtype) for x in own]
        + [
            pltpu.VMEM((PIECES, LOCAL_VARS, PATCH, 512), BF16),
            pltpu.VMEM((GROUPS, 8, SENT_LANES), BF16),
            pltpu.VMEM((GROUPS, 8, SENT_LANES), BF16),
            pltpu.VMEM((PATCH, HEADS, 128), F32),
            pltpu.VMEM((KDIM, HEADS * 128), BF16),
            pltpu.VMEM((HEADS, 128), F32),
            pltpu.VMEM((CELLS, KDIM), F32),
            pltpu.VMEM((HEADS * CELLS, 128), BF16),
            pltpu.VMEM((4, QUAD, D), BF16),
            pltpu.VMEM((4, QUAD, D), BF16),
            pltpu.VMEM((4, QUAD, D), BF16),
            pltpu.VMEM((4, QUAD, D), BF16),
            pltpu.VMEM((2, QUAD, D), BF16),
            pltpu.VMEM((2, QUAD, D), BF16),
            pltpu.SemaphoreType.DMA((GROUPS,)),
            pltpu.SemaphoreType.DMA((GROUPS,)),
            pltpu.SemaphoreType.DMA((8,)),
            pltpu.SemaphoreType.DMA((8,)),
            pltpu.SemaphoreType.DMA((len(operands) + 1,)),
        ],
        compiler_params=pltpu.CompilerParams(
            collective_id=0, has_side_effects=True, vmem_limit_bytes=56 * 1024 * 1024
        ),
        name="forecast_step",
    )(*operands)
    return out.reshape(ROWS, COLS, LEV, VARS * PATCH).transpose(2, 0, 1, 3)


def solution(mesh):
    return jax.shard_map(
        per_device,
        mesh=mesh,
        in_specs=(P(("var", "lat"), None, None, "lon", None),) + (P(),) * 12,
        out_specs=P(None, ("var", "lat"), "lon", None),
        check_vma=False,
    )
```

```python
import functools

import jax
import jax.numpy as jnp
import numpy as np
from jax import lax
from jax.experimental import pallas as pl
from jax.experimental.pallas import tpu as pltpu
from jax.sharding import PartitionSpec as P

MESH = pl.DeviceIdType.MESH
EPSILON = 1e-05
F32 = jnp.float32
BF16 = jnp.bfloat16

GROUPS = 16
LONS = 16
LEV, ROWS, COLS = 2, 6, 12
CELLS = LEV * ROWS * COLS
HALF = CELLS // 2
LOCAL_VARS, PATCH, HEADS, HEAD_DIM = 3, 16, 8, 64
VARS = GROUPS * LOCAL_VARS
OWN = LOCAL_VARS * PATCH
D, FF = 512, 2048
PIECES = 18
WIDE = PIECES * OWN
SENT_LANES = 896
SLOT = 64
KDIM = GROUPS * SLOT
QUAD = 48
QUAD_CELLS = 36
SENT = 40


def cell_index(row, col, lev):
    return (row * COLS + col) * LEV + lev


def band_selector():
    out = np.zeros((GROUPS * 8, 4 * 128), np.float32)
    for band in range(GROUPS):
        for row in range(ROWS):
            out[band * 8 + row, band * ROWS + row] = 1
        for j in range(3):
            out[band * 8 + 6, 128 * (1 + j) + band * ROWS + j] = 1
            out[band * 8 + 7, 128 * (1 + j) + band * ROWS + 3 + j] = 1
    return out


def cell_selector():
    out = np.zeros((CELLS, CELLS), np.float32)
    for piece in range(PIECES):
        for k in range(8):
            if k < 6:
                pair, row = piece, k
            else:
                pair, row = PIECES + piece % 6, 3 * (k - 6) + piece // 6
            out[cell_index(row, pair % COLS, pair // COLS), piece * 8 + k] = 1
    return out


def quad_selector():
    out = np.zeros((4 * QUAD, CELLS), np.float32)
    for row in range(ROWS):
        for col in range(COLS):
            for lev in range(LEV):
                quad = (row // 3) * 2 + col // 6
                place = ((row % 3) * 6 + col % 6) * LEV + lev
                out[quad * QUAD + place, cell_index(row, col, lev)] = 1
    return out


def weight_spread():
    out = np.zeros((128, KDIM), np.float32)
    for group in range(GROUPS):
        for var in range(LOCAL_VARS):
            v, at = group * LOCAL_VARS + var, group * SLOT
            out[v, at + var * PATCH : at + (var + 1) * PATCH] = 1
            out[v, at + 48 + var] = 1
            out[v, at + 51 + var] = 1
    return out


def dot(a, b):
    return jnp.dot(a, b, preferred_element_type=F32)


def dot_t(a, b):
    return lax.dot_general(a, b, (((1,), (1,)), ((), ())), preferred_element_type=F32)


def iota(shape, dim):
    return lax.broadcasted_iota(jnp.int32, shape, dim)


def layer_norm(values, gain):
    shifted = values - jnp.mean(values, axis=-1, keepdims=True)
    spread = jnp.mean(shifted * shifted, axis=-1, keepdims=True)
    return shifted * lax.rsqrt(spread + EPSILON) * gain


def own_lanes(stacked, rows):
    head = iota((rows, 256), 1) // HEAD_DIM
    out = stacked[0:rows]
    for a in range(1, 4):
        out = jnp.where(head == a, stacked[a * rows : (a + 1) * rows], out)
    return out


def attention_four(q, k, v, allowed):
    rows = q.shape[0]
    head = iota((rows, 256), 1) // HEAD_DIM
    scaled = q * jnp.asarray(0.125, BF16)
    none = jnp.zeros_like(scaled)
    stacked = jnp.concatenate([jnp.where(head == a, scaled, none) for a in range(4)], axis=0)
    scores = dot_t(stacked, k)
    probs = []
    for a in range(4):
        part = scores[a * rows : (a + 1) * rows]
        if allowed is not None:
            part = jnp.where(allowed, part, -jnp.inf)
        raised = jnp.exp(part - jnp.max(part, axis=-1, keepdims=True))
        probs.append((raised * (1.0 / jnp.sum(raised, axis=-1, keepdims=True))).astype(BF16))
    return own_lanes(dot(jnp.concatenate(probs, axis=0), v), rows).astype(BF16)


def body(
    fields_hbm,
    band_sel_hbm,
    score_tab_hbm,
    score_bias_hbm,
    value_bias_hbm,
    value_tab_hbm,
    spread_hbm,
    cell_sel_hbm,
    agg_hbm,
    gains_hbm,
    qkv_hbm,
    proj_hbm,
    up_hbm,
    down_hbm,
    quad_sel_hbm,
    quad_back_hbm,
    decode_hbm,
    decode_bias_hbm,
    out_ref,
    fields,
    band_sel,
    score_tab,
    score_bias,
    value_bias,
    table,
    spread,
    cell_sel,
    agg,
    gains,
    qkv_w,
    proj_w,
    up_w,
    down_w,
    quad_sel,
    quad_back,
    decode_w,
    decode_bias,
    lifted,
    outgoing,
    incoming,
    score_wide,
    score_w,
    bias_wide,
    raw,
    weights_all,
    quads,
    window,
    context,
    returned,
    edge,
    edge_context,
    send_sem,
    recv_sem,
    halo_send,
    halo_recv,
    load_sem,
):
    var, lon, lat = lax.axis_index("var"), lax.axis_index("lon"), lax.axis_index("lat")
    band = var * 2 + lat
    up_band, down_band = lax.rem(band + GROUPS - 1, GROUPS), lax.rem(band + 1, GROUPS)
    left, right = lax.rem(lon + LONS - 1, LONS), lax.rem(lon + 1, LONS)

    def device(of_band, of_lon):
        return (of_band // 2, of_lon, lax.rem(of_band, 2))

    loads = {
        "fields": (fields_hbm, fields),
        "band_sel": (band_sel_hbm, band_sel),
        "score_tab": (score_tab_hbm, score_tab),
        "score_bias": (score_bias_hbm, score_bias),
        "value_bias": (value_bias_hbm, value_bias),
        "table": (value_tab_hbm, table.at[:, 0:OWN, :]),
        "spread": (spread_hbm, spread),
        "cell_sel": (cell_sel_hbm, cell_sel),
        "agg": (agg_hbm, agg),
        "gains": (gains_hbm, gains),
        "qkv0": (qkv_hbm.at[0], qkv_w.at[0]),
        "proj": (proj_hbm, proj_w),
        "up": (up_hbm, up_w),
        "down": (down_hbm, down_w),
        "quad_sel": (quad_sel_hbm, quad_sel),
        "qkv1": (qkv_hbm.at[1], qkv_w.at[1]),
        "quad_back": (quad_back_hbm, quad_back),
        "decode": (decode_hbm, decode_w),
        "decode_bias": (decode_bias_hbm, decode_bias),
    }
    loads = {
        name: pltpu.make_async_copy(a, b, load_sem.at[i]) for i, (name, (a, b)) in enumerate(loads.items())
    }
    loads["fields"].start()
    loads["band_sel"].start()

    barrier = pltpu.get_barrier_semaphore()
    peers = [device(lax.rem(band + k, GROUPS), lon) for k in range(1, GROUPS)]
    peers += [device(up_band, left), device(band, left), device(down_band, right), device(band, right)]
    for peer in peers:
        pl.semaphore_signal(barrier, inc=1, device_id=peer, device_id_type=MESH)

    lifted[...] = jnp.zeros(lifted.shape, BF16)
    loads["fields"].wait()
    loads["band_sel"].wait()
    rows = GROUPS * ROWS
    half = COLS // 2
    for v in range(LOCAL_VARS):
        lifted[0:COLS, v, :, 0:rows] = fields[v, 0]
        lifted[COLS:PIECES, v, :, 0:rows] = fields[v, 1, 0:half]
        for j in range(3):
            lifted[6 * j : 6 * j + 6, v, :, 128 * (1 + j) : 128 * (1 + j) + rows] = fields[v, 1, half:COLS]
    turned = dot_t(band_sel[...], lifted[...].reshape(WIDE, 512))
    outgoing[:, :, 0:WIDE] = turned.reshape(GROUPS, 8, WIDE).astype(BF16)

    pl.semaphore_wait(barrier, len(peers))

    sends = []
    for k in range(1, GROUPS):
        to = k - 1 + (k - 1 >= band).astype(jnp.int32)
        copy = pltpu.make_async_remote_copy(
            src_ref=outgoing.at[to],
            dst_ref=incoming.at[band],
            send_sem=send_sem.at[k],
            recv_sem=recv_sem.at[band],
            device_id=device(to, lon),
            device_id_type=MESH,
        )
        copy.start()
        sends.append(copy)
    own = pltpu.make_async_copy(outgoing.at[band], incoming.at[band], send_sem.at[0])
    own.start()
    for name, load in loads.items():
        if name not in ("fields", "band_sel"):
            load.start()

    shape = (GROUPS, 4, PATCH, 128)
    part = iota(shape, 1)
    match = (3 * iota(shape, 0) + part == iota(shape, 3)) & (part < 3)
    score_wide[...] = jnp.zeros(score_wide.shape, F32)
    bias_wide[...] = jnp.zeros(bias_wide.shape, F32)
    loads["score_tab"].wait()
    score_wide[:, :, 0:VARS] = score_tab[...].astype(F32)
    for h in range(HEADS):
        tab = jnp.broadcast_to(score_wide[:, h, :][None, None], shape)
        score_w[:, h * 128 : (h + 1) * 128] = jnp.where(match, tab, 0.0).reshape(KDIM, 128).astype(BF16)
    loads["score_bias"].wait()
    bias_wide[:, 0:VARS] = score_bias[...]
    loads["value_bias"].wait()
    bias = value_bias[...]
    bias_high = bias.astype(BF16)
    bias_low = (bias - bias_high.astype(F32)).astype(BF16)
    at_row, at_var = iota((GROUPS * 8, VARS), 0), iota((GROUPS * 8, VARS), 1)
    kind, first = at_row % 8, 3 * (at_row // 8)
    high = jnp.where((kind < 3) & (at_var == first + kind), 1.0, 0.0).astype(BF16)
    low = jnp.where((kind > 2) & (kind < 6) & (at_var == first + kind - 3), 1.0, 0.0).astype(BF16)
    bias_rows = dot(high, bias_high) + dot(low, bias_low)
    table[:, OWN : OWN + 8, :] = bias_rows.reshape(GROUPS, 8, D).astype(BF16)
    table[:, OWN + 8 : SLOT, :] = jnp.zeros((GROUPS, 8, D), BF16)
    window[:, SENT:QUAD, :] = jnp.zeros((4, QUAD - SENT, D), BF16)
    returned[:, SENT:QUAD, :] = jnp.zeros((4, QUAD - SENT, D), BF16)
    edge[:, SENT:QUAD, :] = jnp.zeros((2, QUAD - SENT, D), BF16)
    first_band, last_band = band == 0, band == GROUPS - 1

    @pl.when(first_band)
    def _():
        window[2:4, 0:SENT, :] = jnp.zeros((2, SENT, D), BF16)

    for name in ("table", "spread", "cell_sel"):
        loads[name].wait()

    own.wait()
    lane = iota((8, 128), 1)
    in_first = lane < OWN
    in_second = (lane >= SLOT) & (lane < SLOT + OWN)
    ones = jnp.where((lane % SLOT >= OWN) & (lane % SLOT < OWN + 6), 1.0, 0.0)
    for j in range(GROUPS // 2):
        for source in (2 * j, 2 * j + 1):
            arrival = pltpu.make_async_remote_copy(
                src_ref=outgoing.at[source],
                dst_ref=incoming.at[source],
                send_sem=send_sem.at[source],
                recv_sem=recv_sem.at[source],
                device_id=device(source, lon),
                device_id_type=MESH,
            )
            pl.when(band != source)(arrival.wait_recv)
        two = [incoming[2 * j].astype(F32), incoming[2 * j + 1].astype(F32)]
        for piece in range(PIECES):
            tile, at = divmod(piece * OWN, 128)
            moved = []
            for side in range(2):
                x = two[side][:, tile * 128 : (tile + 1) * 128]
                if at + OWN > 128:
                    x = jnp.where(lane >= at, x, two[side][:, (tile + 1) * 128 : (tile + 2) * 128])
                shift = (SLOT * side - at) % 128
                moved.append(pltpu.roll(x, shift, 1) if shift else x)
            raw[8 * piece : 8 * piece + 8, j * 128 : (j + 1) * 128] = jnp.where(
                in_first, moved[0], jnp.where(in_second, moved[1], ones)
            )
    cells = raw[...].astype(BF16)

    real = iota((CELLS, 128), 1) < VARS
    totals = []
    for h in range(HEADS):
        if h % 2 == 0:
            both = dot(cells, score_w[:, h * 128 : (h + 2) * 128])
        scores = both[:, h % 2 * 128 : (h % 2 + 1) * 128] + bias_wide[h : h + 1, :]
        scores = jnp.where(real, scores, -jnp.inf)
        weights = jnp.exp(scores - jnp.max(scores, axis=-1, keepdims=True)).astype(BF16)
        totals.append(1.0 / jnp.sum(weights.astype(F32), axis=-1, keepdims=True))
        weights_all[h * CELLS : (h + 1) * CELLS, :] = weights
    all_table = table[...].reshape(KDIM, D)
    groups = []
    for g in range(2):
        own_weights = weights_all[4 * g * CELLS : 4 * (g + 1) * CELLS, :]
        sums = None
        for t in range(KDIM // 256):
            at = slice(t * 256, (t + 1) * 256)
            spread_w = dot(own_weights, spread[:, at]).astype(BF16)
            repeated = jnp.concatenate([cells[:, at]] * 4, axis=0)
            more = dot(repeated * spread_w, all_table[at, g * 256 : (g + 1) * 256])
            sums = more if sums is None else sums + more
        scaled = [sums[a * CELLS : (a + 1) * CELLS] * totals[4 * g + a] for a in range(4)]
        groups.append(own_lanes(jnp.concatenate(scaled, axis=0), CELLS).astype(BF16))
    pooled = jnp.concatenate(groups, axis=1)
    pooled = dot(cell_sel[...], pooled).astype(BF16)

    loads["agg"].wait()
    latent = dot(pooled, agg[...])

    loads["gains"].wait()
    normed = layer_norm(latent, gains[0:1, :]).astype(BF16)
    loads["qkv0"].wait()
    qkv = dot(normed, qkv_w[0]).astype(BF16)
    mixed = jnp.concatenate(
        [
            attention_four(
                qkv[:, at : at + 256], qkv[:, D + at : D + at + 256], qkv[:, 2 * D + at : 2 * D + at + 256], None
            )
            for at in (0, 256)
        ],
        axis=1,
    )
    loads["proj"].wait()
    hidden = latent + dot(mixed, proj_w[0])

    loads["up"].wait()
    loads["down"].wait()
    loads["quad_sel"].wait()

    def halo(source, target, sent, arrived, to):
        return pltpu.make_async_remote_copy(
            src_ref=source,
            dst_ref=target,
            send_sem=halo_send.at[sent],
            recv_sem=halo_recv.at[arrived],
            device_id=to,
            device_id_type=MESH,
        )

    rows = slice(0, SENT)
    out_right = halo(quads.at[1, rows], window.at[1, rows], 0, 0, device(band, right))
    out_down = halo(quads.at[2, rows], window.at[2, rows], 1, 1, device(down_band, lon))
    out_corner = halo(quads.at[3, rows], window.at[3, rows], 2, 2, device(down_band, right))
    out_edge = halo(quads.at[3, rows], edge.at[1, rows], 3, 3, device(band, right))
    back_left = halo(context.at[1, rows], returned.at[1, rows], 4, 4, device(band, left))
    back_up = halo(context.at[2, rows], returned.at[2, rows], 5, 5, device(up_band, lon))
    back_corner = halo(context.at[3, rows], returned.at[3, rows], 6, 6, device(up_band, left))
    back_edge = halo(edge_context.at[1, rows], returned.at[3, rows], 7, 6, device(band, left))

    ended = [None, None]
    for lower in (1, 0):
        latent = hidden[lower * HALF : (lower + 1) * HALF]
        mixed = layer_norm(latent, gains[1:2, :]).astype(BF16)
        for j in range(FF // D):
            at = slice(j * D, (j + 1) * D)
            active = jax.nn.gelu(dot(mixed, up_w[:, at]), approximate=True).astype(BF16)
            latent = latent + dot(active, down_w[at, :])
        ended[lower] = latent
        normed = layer_norm(latent, gains[2:3, :]).astype(BF16)
        quads[2 * lower : 2 * lower + 2] = dot(quad_sel[...], normed).astype(BF16).reshape(2, QUAD, D)
        if lower:

            @pl.when(jnp.logical_not(last_band))
            def _():
                out_corner.start()
                out_down.start()

            @pl.when(last_band)
            def _():
                out_edge.start()
                edge[0] = quads[2]

    out_right.start()
    window[0] = quads[0]
    latent = jnp.concatenate(ended, axis=0)
    at_query, at_key = iota((4 * QUAD, 4 * QUAD), 0), iota((4 * QUAD, 4 * QUAD), 1)
    same_level = (at_query % 2 == at_key % 2) & (at_key % QUAD < QUAD_CELLS)
    same_half = (at_query < 2 * QUAD) == (at_key < 2 * QUAD)
    allowed = same_level & (same_half | jnp.logical_not(first_band))
    for name in ("qkv1", "quad_back", "decode", "decode_bias"):
        loads[name].wait()

    def window_context(cells_in, out, mask):
        count = 4 if out is context else 2
        qkv = dot(cells_in[...].reshape(count * QUAD, D), qkv_w[1]).astype(BF16)
        for at in (0, 256):
            out[:, :, at : at + 256] = attention_four(
                qkv[:, at : at + 256], qkv[:, D + at : D + at + 256], qkv[:, 2 * D + at : 2 * D + at + 256], mask
            ).reshape(count, QUAD, 256)

    out_right.wait_recv()

    @pl.when(jnp.logical_not(first_band))
    def _():
        out_down.wait_recv()
        out_corner.wait_recv()

    window_context(window, context, allowed)

    @pl.when(jnp.logical_not(first_band))
    def _():
        back_corner.start()
        back_up.start()

    back_left.start()
    returned[0] = context[0]

    @pl.when(last_band)
    def _():
        out_edge.wait_recv()
        window_context(edge, edge_context, same_level[0 : 2 * QUAD, 0 : 2 * QUAD])
        back_edge.start()
        returned[2] = edge_context[0]

    back_left.wait_recv()
    back_corner.wait_recv()

    @pl.when(jnp.logical_not(last_band))
    def _():
        back_up.wait_recv()

    mixed = dot(quad_back[...], returned[...].reshape(4 * QUAD, D)).astype(BF16)
    latent = latent + dot(mixed, proj_w[1])
    final = layer_norm(latent, gains[3:4, :]).astype(BF16)
    offsets = jnp.concatenate([decode_bias[i : i + 1, :] for i in range(VARS * PATCH // 128)], axis=1)
    out_ref[...] = (dot(final, decode_w[...]) + offsets).astype(BF16).reshape(CELLS // LEV, LEV, VARS * PATCH)

    for copy in sends + [out_right, back_left]:
        copy.wait_send()

    @pl.when(jnp.logical_not(last_band))
    def _():
        out_down.wait_send()
        out_corner.wait_send()

    @pl.when(jnp.logical_not(first_band))
    def _():
        back_up.wait_send()
        back_corner.wait_send()

    @pl.when(last_band)
    def _():
        out_edge.wait_send()
        back_edge.wait_send()


def per_device(
    fields,
    score_table,
    score_bias,
    value_table,
    value_bias,
    agg_weight,
    qkv_weight,
    proj_weight,
    up_weight,
    down_weight,
    norm_gains,
    decode_weight,
    decode_bias,
):
    quads = quad_selector()
    operands = [
        fields.transpose(0, 1, 3, 4, 2),
        jnp.asarray(band_selector(), BF16),
        score_table.transpose(1, 2, 0),
        score_bias.T,
        value_bias,
        value_table.reshape(GROUPS, OWN, D),
        jnp.asarray(weight_spread(), BF16),
        jnp.asarray(cell_selector(), BF16),
        agg_weight,
        norm_gains,
        qkv_weight,
        proj_weight,
        up_weight,
        down_weight,
        jnp.asarray(quads[0 : 2 * QUAD, 0:HALF], BF16),
        jnp.asarray(quads.T, BF16),
        decode_weight,
        decode_bias.reshape(-1, 128),
    ]
    own = [jax.ShapeDtypeStruct(x.shape, x.dtype) for x in operands]
    own[5] = jax.ShapeDtypeStruct((GROUPS, SLOT, D), BF16)
    out = pl.pallas_call(
        body,
        out_shape=pltpu.VMEM((CELLS // LEV, LEV, VARS * PATCH), BF16),
        in_specs=[pl.BlockSpec(memory_space=pl.ANY)] * len(operands),
        out_specs=pl.BlockSpec(memory_space=pltpu.VMEM),
        scratch_shapes=[pltpu.VMEM(x.shape, x.dtype) for x in own]
        + [
            pltpu.VMEM((PIECES, LOCAL_VARS, PATCH, 512), BF16),
            pltpu.VMEM((GROUPS, 8, SENT_LANES), BF16),
            pltpu.VMEM((GROUPS, 8, SENT_LANES), BF16),
            pltpu.VMEM((PATCH, HEADS, 128), F32),
            pltpu.VMEM((KDIM, HEADS * 128), BF16),
            pltpu.VMEM((HEADS, 128), F32),
            pltpu.VMEM((CELLS, KDIM), F32),
            pltpu.VMEM((HEADS * CELLS, 128), BF16),
            pltpu.VMEM((4, QUAD, D), BF16),
            pltpu.VMEM((4, QUAD, D), BF16),
            pltpu.VMEM((4, QUAD, D), BF16),
            pltpu.VMEM((4, QUAD, D), BF16),
            pltpu.VMEM((2, QUAD, D), BF16),
            pltpu.VMEM((2, QUAD, D), BF16),
            pltpu.SemaphoreType.DMA((GROUPS,)),
            pltpu.SemaphoreType.DMA((GROUPS,)),
            pltpu.SemaphoreType.DMA((8,)),
            pltpu.SemaphoreType.DMA((8,)),
            pltpu.SemaphoreType.DMA((len(operands) + 1,)),
        ],
        compiler_params=pltpu.CompilerParams(
            collective_id=0, has_side_effects=True, vmem_limit_bytes=56 * 1024 * 1024
        ),
        name="forecast_step",
    )(*operands)
    return out.reshape(ROWS, COLS, LEV, VARS * PATCH).transpose(2, 0, 1, 3)


def solution(mesh):
    return jax.shard_map(
        per_device,
        mesh=mesh,
        in_specs=(P(("var", "lat"), None, None, "lon", None),) + (P(),) * 12,
        out_specs=P(None, ("var", "lat"), "lon", None),
        check_vma=False,
    )
```

```python
import functools

import jax
import jax.numpy as jnp
import numpy as np
from jax import lax
from jax.experimental import pallas as pl
from jax.experimental.pallas import tpu as pltpu
from jax.sharding import PartitionSpec as P

MESH = pl.DeviceIdType.MESH
EPSILON = 1e-05
F32 = jnp.float32
BF16 = jnp.bfloat16

GROUPS = 16
LONS = 16
LEV, ROWS, COLS = 2, 6, 12
CELLS = LEV * ROWS * COLS
HALF = CELLS // 2
LOCAL_VARS, PATCH, HEADS, HEAD_DIM = 3, 16, 8, 64
VARS = GROUPS * LOCAL_VARS
OWN = LOCAL_VARS * PATCH
D, FF = 512, 2048
PIECES = 18
WIDE = PIECES * OWN
SENT_LANES = 896
SLOT = 64
KDIM = GROUPS * SLOT
QUAD = 48
QUAD_CELLS = 36
SENT = 40


def cell_index(row, col, lev):
    return (row * COLS + col) * LEV + lev


def band_selector():
    out = np.zeros((GROUPS * 8, 4 * 128), np.float32)
    for band in range(GROUPS):
        for row in range(ROWS):
            out[band * 8 + row, band * ROWS + row] = 1
        for j in range(3):
            out[band * 8 + 6, 128 * (1 + j) + band * ROWS + j] = 1
            out[band * 8 + 7, 128 * (1 + j) + band * ROWS + 3 + j] = 1
    return out


def cell_selector():
    out = np.zeros((CELLS, CELLS), np.float32)
    for piece in range(PIECES):
        for k in range(8):
            if k < 6:
                pair, row = piece, k
            else:
                pair, row = PIECES + piece % 6, 3 * (k - 6) + piece // 6
            out[cell_index(row, pair % COLS, pair // COLS), piece * 8 + k] = 1
    return out


def quad_selector():
    out = np.zeros((4 * QUAD, CELLS), np.float32)
    for row in range(ROWS):
        for col in range(COLS):
            for lev in range(LEV):
                quad = (row // 3) * 2 + col // 6
                place = ((row % 3) * 6 + col % 6) * LEV + lev
                out[quad * QUAD + place, cell_index(row, col, lev)] = 1
    return out


def weight_spread():
    out = np.zeros((128, KDIM), np.float32)
    for group in range(GROUPS):
        for var in range(LOCAL_VARS):
            v, at = group * LOCAL_VARS + var, group * SLOT
            out[v, at + var * PATCH : at + (var + 1) * PATCH] = 1
            out[v, at + 48 + var] = 1
            out[v, at + 51 + var] = 1
    return out


def dot(a, b):
    return jnp.dot(a, b, preferred_element_type=F32)


def dot_t(a, b):
    return lax.dot_general(a, b, (((1,), (1,)), ((), ())), preferred_element_type=F32)


def iota(shape, dim):
    return lax.broadcasted_iota(jnp.int32, shape, dim)


def layer_norm(values, gain):
    shifted = values - jnp.mean(values, axis=-1, keepdims=True)
    spread = jnp.mean(shifted * shifted, axis=-1, keepdims=True)
    return shifted * lax.rsqrt(spread + EPSILON) * gain


def own_lanes(stacked, rows):
    head = iota((rows, 256), 1) // HEAD_DIM
    out = stacked[0:rows]
    for a in range(1, 4):
        out = jnp.where(head == a, stacked[a * rows : (a + 1) * rows], out)
    return out


def attention_four(q, k, v, allowed):
    rows = q.shape[0]
    head = iota((rows, 256), 1) // HEAD_DIM
    scaled = q * jnp.asarray(0.125, BF16)
    none = jnp.zeros_like(scaled)
    stacked = jnp.concatenate([jnp.where(head == a, scaled, none) for a in range(4)], axis=0)
    scores = dot_t(stacked, k)
    probs = []
    for a in range(4):
        part = scores[a * rows : (a + 1) * rows]
        if allowed is not None:
            part = jnp.where(allowed, part, -jnp.inf)
        raised = jnp.exp(part - jnp.max(part, axis=-1, keepdims=True))
        probs.append((raised * (1.0 / jnp.sum(raised, axis=-1, keepdims=True))).astype(BF16))
    return own_lanes(dot(jnp.concatenate(probs, axis=0), v), rows).astype(BF16)


def body(
    fields_hbm,
    band_sel_hbm,
    score_tab_hbm,
    score_bias_hbm,
    value_bias_hbm,
    value_tab_hbm,
    spread_hbm,
    cell_sel_hbm,
    agg_hbm,
    gains_hbm,
    qkv_hbm,
    proj_hbm,
    up_hbm,
    down_hbm,
    quad_sel_hbm,
    quad_back_hbm,
    decode_hbm,
    decode_bias_hbm,
    out_ref,
    fields,
    band_sel,
    score_tab,
    score_bias,
    value_bias,
    table,
    spread,
    cell_sel,
    agg,
    gains,
    qkv_w,
    proj_w,
    up_w,
    down_w,
    quad_sel,
    quad_back,
    decode_w,
    decode_bias,
    lifted,
    outgoing,
    incoming,
    score_wide,
    score_w,
    bias_wide,
    raw,
    weights_all,
    quads,
    window,
    context,
    returned,
    edge,
    edge_context,
    send_sem,
    recv_sem,
    halo_send,
    halo_recv,
    load_sem,
):
    var, lon, lat = lax.axis_index("var"), lax.axis_index("lon"), lax.axis_index("lat")
    band = var * 2 + lat
    up_band, down_band = lax.rem(band + GROUPS - 1, GROUPS), lax.rem(band + 1, GROUPS)
    left, right = lax.rem(lon + LONS - 1, LONS), lax.rem(lon + 1, LONS)

    def device(of_band, of_lon):
        return (of_band // 2, of_lon, lax.rem(of_band, 2))

    loads = {
        "fields": (fields_hbm, fields),
        "band_sel": (band_sel_hbm, band_sel),
        "score_tab": (score_tab_hbm, score_tab),
        "score_bias": (score_bias_hbm, score_bias),
        "value_bias": (value_bias_hbm, value_bias),
        "table": (value_tab_hbm, table.at[:, 0:OWN, :]),
        "spread": (spread_hbm, spread),
        "cell_sel": (cell_sel_hbm, cell_sel),
        "agg": (agg_hbm, agg),
        "gains": (gains_hbm, gains),
        "qkv0": (qkv_hbm.at[0], qkv_w.at[0]),
        "proj": (proj_hbm, proj_w),
        "up": (up_hbm, up_w),
        "down": (down_hbm, down_w),
        "quad_sel": (quad_sel_hbm, quad_sel),
        "qkv1": (qkv_hbm.at[1], qkv_w.at[1]),
        "quad_back": (quad_back_hbm, quad_back),
        "decode": (decode_hbm, decode_w),
        "decode_bias": (decode_bias_hbm, decode_bias),
    }
    loads = {
        name: pltpu.make_async_copy(a, b, load_sem.at[i]) for i, (name, (a, b)) in enumerate(loads.items())
    }
    loads["fields"].start()
    loads["band_sel"].start()

    barrier = pltpu.get_barrier_semaphore()
    peers = [device(lax.rem(band + k, GROUPS), lon) for k in range(1, GROUPS)]
    peers += [device(up_band, left), device(band, left), device(down_band, right), device(band, right)]
    for peer in peers:
        pl.semaphore_signal(barrier, inc=1, device_id=peer, device_id_type=MESH)

    lifted[...] = jnp.zeros(lifted.shape, BF16)
    loads["fields"].wait()
    loads["band_sel"].wait()
    rows = GROUPS * ROWS
    half = COLS // 2
    for v in range(LOCAL_VARS):
        lifted[0:COLS, v, :, 0:rows] = fields[v, 0]
        lifted[COLS:PIECES, v, :, 0:rows] = fields[v, 1, 0:half]
        for j in range(3):
            lifted[6 * j : 6 * j + 6, v, :, 128 * (1 + j) : 128 * (1 + j) + rows] = fields[v, 1, half:COLS]

    def turn(first, count):
        turned = dot_t(band_sel[first * 8 : (first + count) * 8, :], lifted[...].reshape(WIDE, 512))
        outgoing[first : first + count, :, 0:WIDE] = turned.reshape(count, 8, WIDE).astype(BF16)

    turn(0, GROUPS // 2)

    pl.semaphore_wait(barrier, len(peers))

    sends = []
    for k in range(1, GROUPS):
        if k == GROUPS // 2:
            turn(GROUPS // 2, GROUPS // 2)
        to = k - 1 + (k - 1 >= band).astype(jnp.int32)
        copy = pltpu.make_async_remote_copy(
            src_ref=outgoing.at[to],
            dst_ref=incoming.at[band],
            send_sem=send_sem.at[k],
            recv_sem=recv_sem.at[band],
            device_id=device(to, lon),
            device_id_type=MESH,
        )
        copy.start()
        sends.append(copy)
    own = pltpu.make_async_copy(outgoing.at[band], incoming.at[band], send_sem.at[0])
    own.start()
    for name, load in loads.items():
        if name not in ("fields", "band_sel"):
            load.start()

    shape = (GROUPS, 4, PATCH, 128)
    part = iota(shape, 1)
    match = (3 * iota(shape, 0) + part == iota(shape, 3)) & (part < 3)
    score_wide[...] = jnp.zeros(score_wide.shape, F32)
    bias_wide[...] = jnp.zeros(bias_wide.shape, F32)
    loads["score_tab"].wait()
    score_wide[:, :, 0:VARS] = score_tab[...].astype(F32)
    for h in range(HEADS):
        tab = jnp.broadcast_to(score_wide[:, h, :][None, None], shape)
        score_w[:, h * 128 : (h + 1) * 128] = jnp.where(match, tab, 0.0).reshape(KDIM, 128).astype(BF16)
    loads["score_bias"].wait()
    bias_wide[:, 0:VARS] = score_bias[...]
    loads["value_bias"].wait()
    bias = value_bias[...]
    bias_high = bias.astype(BF16)
    bias_low = (bias - bias_high.astype(F32)).astype(BF16)
    at_row, at_var = iota((GROUPS * 8, VARS), 0), iota((GROUPS * 8, VARS), 1)
    kind, first = at_row % 8, 3 * (at_row // 8)
    high = jnp.where((kind < 3) & (at_var == first + kind), 1.0, 0.0).astype(BF16)
    low = jnp.where((kind > 2) & (kind < 6) & (at_var == first + kind - 3), 1.0, 0.0).astype(BF16)
    bias_rows = dot(high, bias_high) + dot(low, bias_low)
    table[:, OWN : OWN + 8, :] = bias_rows.reshape(GROUPS, 8, D).astype(BF16)
    table[:, OWN + 8 : SLOT, :] = jnp.zeros((GROUPS, 8, D), BF16)
    window[:, SENT:QUAD, :] = jnp.zeros((4, QUAD - SENT, D), BF16)
    returned[:, SENT:QUAD, :] = jnp.zeros((4, QUAD - SENT, D), BF16)
    edge[:, SENT:QUAD, :] = jnp.zeros((2, QUAD - SENT, D), BF16)
    first_band, last_band = band == 0, band == GROUPS - 1

    @pl.when(first_band)
    def _():
        window[2:4, 0:SENT, :] = jnp.zeros((2, SENT, D), BF16)

    for name in ("table", "spread", "cell_sel"):
        loads[name].wait()

    own.wait()
    lane = iota((8, 128), 1)
    in_first = lane < OWN
    in_second = (lane >= SLOT) & (lane < SLOT + OWN)
    ones = jnp.where((lane % SLOT >= OWN) & (lane % SLOT < OWN + 6), 1.0, 0.0)
    for j in range(GROUPS // 2):
        for source in (2 * j, 2 * j + 1):
            arrival = pltpu.make_async_remote_copy(
                src_ref=outgoing.at[source],
                dst_ref=incoming.at[source],
                send_sem=send_sem.at[source],
                recv_sem=recv_sem.at[source],
                device_id=device(source, lon),
                device_id_type=MESH,
            )
            pl.when(band != source)(arrival.wait_recv)
        two = [incoming[2 * j].astype(F32), incoming[2 * j + 1].astype(F32)]
        for piece in range(PIECES):
            tile, at = divmod(piece * OWN, 128)
            moved = []
            for side in range(2):
                x = two[side][:, tile * 128 : (tile + 1) * 128]
                if at + OWN > 128:
                    x = jnp.where(lane >= at, x, two[side][:, (tile + 1) * 128 : (tile + 2) * 128])
                shift = (SLOT * side - at) % 128
                moved.append(pltpu.roll(x, shift, 1) if shift else x)
            raw[8 * piece : 8 * piece + 8, j * 128 : (j + 1) * 128] = jnp.where(
                in_first, moved[0], jnp.where(in_second, moved[1], ones)
            )
    cells = raw[...].astype(BF16)

    real = iota((CELLS, 128), 1) < VARS
    totals = []
    for h in range(HEADS):
        if h % 2 == 0:
            both = dot(cells, score_w[:, h * 128 : (h + 2) * 128])
        scores = both[:, h % 2 * 128 : (h % 2 + 1) * 128] + bias_wide[h : h + 1, :]
        scores = jnp.where(real, scores, -jnp.inf)
        weights = jnp.exp(scores - jnp.max(scores, axis=-1, keepdims=True)).astype(BF16)
        totals.append(1.0 / jnp.sum(weights.astype(F32), axis=-1, keepdims=True))
        weights_all[h * CELLS : (h + 1) * CELLS, :] = weights
    all_table = table[...].reshape(KDIM, D)
    groups = []
    for g in range(2):
        own_weights = weights_all[4 * g * CELLS : 4 * (g + 1) * CELLS, :]
        sums = None
        for t in range(KDIM // 256):
            at = slice(t * 256, (t + 1) * 256)
            spread_w = dot(own_weights, spread[:, at]).astype(BF16)
            repeated = jnp.concatenate([cells[:, at]] * 4, axis=0)
            more = dot(repeated * spread_w, all_table[at, g * 256 : (g + 1) * 256])
            sums = more if sums is None else sums + more
        scaled = [sums[a * CELLS : (a + 1) * CELLS] * totals[4 * g + a] for a in range(4)]
        groups.append(own_lanes(jnp.concatenate(scaled, axis=0), CELLS).astype(BF16))
    pooled = jnp.concatenate(groups, axis=1)
    pooled = dot(cell_sel[...], pooled).astype(BF16)

    loads["agg"].wait()
    latent = dot(pooled, agg[...])

    loads["gains"].wait()
    normed = layer_norm(latent, gains[0:1, :]).astype(BF16)
    loads["qkv0"].wait()
    qkv = dot(normed, qkv_w[0]).astype(BF16)
    mixed = jnp.concatenate(
        [
            attention_four(
                qkv[:, at : at + 256], qkv[:, D + at : D + at + 256], qkv[:, 2 * D + at : 2 * D + at + 256], None
            )
            for at in (0, 256)
        ],
        axis=1,
    )
    loads["proj"].wait()
    hidden = latent + dot(mixed, proj_w[0])

    loads["up"].wait()
    loads["down"].wait()
    loads["quad_sel"].wait()

    def halo(source, target, sent, arrived, to):
        return pltpu.make_async_remote_copy(
            src_ref=source,
            dst_ref=target,
            send_sem=halo_send.at[sent],
            recv_sem=halo_recv.at[arrived],
            device_id=to,
            device_id_type=MESH,
        )

    rows = slice(0, SENT)
    out_right = halo(quads.at[1, rows], window.at[1, rows], 0, 0, device(band, right))
    out_down = halo(quads.at[2, rows], window.at[2, rows], 1, 1, device(down_band, lon))
    out_corner = halo(quads.at[3, rows], window.at[3, rows], 2, 2, device(down_band, right))
    out_edge = halo(quads.at[3, rows], edge.at[1, rows], 3, 3, device(band, right))
    back_left = halo(context.at[1, rows], returned.at[1, rows], 4, 4, device(band, left))
    back_up = halo(context.at[2, rows], returned.at[2, rows], 5, 5, device(up_band, lon))
    back_corner = halo(context.at[3, rows], returned.at[3, rows], 6, 6, device(up_band, left))
    back_edge = halo(edge_context.at[1, rows], returned.at[3, rows], 7, 6, device(band, left))

    ended = [None, None]
    for lower in (1, 0):
        latent = hidden[lower * HALF : (lower + 1) * HALF]
        mixed = layer_norm(latent, gains[1:2, :]).astype(BF16)
        for j in range(FF // D):
            at = slice(j * D, (j + 1) * D)
            active = jax.nn.gelu(dot(mixed, up_w[:, at]), approximate=True).astype(BF16)
            latent = latent + dot(active, down_w[at, :])
        ended[lower] = latent
        normed = layer_norm(latent, gains[2:3, :]).astype(BF16)
        quads[2 * lower : 2 * lower + 2] = dot(quad_sel[...], normed).astype(BF16).reshape(2, QUAD, D)
        if lower:

            @pl.when(jnp.logical_not(last_band))
            def _():
                out_corner.start()
                out_down.start()

            @pl.when(last_band)
            def _():
                out_edge.start()
                edge[0] = quads[2]

    out_right.start()
    window[0] = quads[0]
    latent = jnp.concatenate(ended, axis=0)
    at_query, at_key = iota((4 * QUAD, 4 * QUAD), 0), iota((4 * QUAD, 4 * QUAD), 1)
    same_level = (at_query % 2 == at_key % 2) & (at_key % QUAD < QUAD_CELLS)
    same_half = (at_query < 2 * QUAD) == (at_key < 2 * QUAD)
    allowed = same_level & (same_half | jnp.logical_not(first_band))
    for name in ("qkv1", "quad_back", "decode", "decode_bias"):
        loads[name].wait()

    def window_context(cells_in, out, mask):
        count = 4 if out is context else 2
        qkv = dot(cells_in[...].reshape(count * QUAD, D), qkv_w[1]).astype(BF16)
        for at in (0, 256):
            out[:, :, at : at + 256] = attention_four(
                qkv[:, at : at + 256], qkv[:, D + at : D + at + 256], qkv[:, 2 * D + at : 2 * D + at + 256], mask
            ).reshape(count, QUAD, 256)

    out_right.wait_recv()

    @pl.when(jnp.logical_not(first_band))
    def _():
        out_down.wait_recv()
        out_corner.wait_recv()

    window_context(window, context, allowed)

    @pl.when(jnp.logical_not(first_band))
    def _():
        back_corner.start()
        back_up.start()

    back_left.start()
    returned[0] = context[0]

    @pl.when(last_band)
    def _():
        out_edge.wait_recv()
        window_context(edge, edge_context, same_level[0 : 2 * QUAD, 0 : 2 * QUAD])
        back_edge.start()
        returned[2] = edge_context[0]

    back_left.wait_recv()
    back_corner.wait_recv()

    @pl.when(jnp.logical_not(last_band))
    def _():
        back_up.wait_recv()

    mixed = dot(quad_back[...], returned[...].reshape(4 * QUAD, D)).astype(BF16)
    latent = latent + dot(mixed, proj_w[1])
    final = layer_norm(latent, gains[3:4, :]).astype(BF16)
    offsets = jnp.concatenate([decode_bias[i : i + 1, :] for i in range(VARS * PATCH // 128)], axis=1)
    out_ref[...] = (dot(final, decode_w[...]) + offsets).astype(BF16).reshape(CELLS // LEV, LEV, VARS * PATCH)

    for copy in sends + [out_right, back_left]:
        copy.wait_send()

    @pl.when(jnp.logical_not(last_band))
    def _():
        out_down.wait_send()
        out_corner.wait_send()

    @pl.when(jnp.logical_not(first_band))
    def _():
        back_up.wait_send()
        back_corner.wait_send()

    @pl.when(last_band)
    def _():
        out_edge.wait_send()
        back_edge.wait_send()


def per_device(
    fields,
    score_table,
    score_bias,
    value_table,
    value_bias,
    agg_weight,
    qkv_weight,
    proj_weight,
    up_weight,
    down_weight,
    norm_gains,
    decode_weight,
    decode_bias,
):
    quads = quad_selector()
    operands = [
        fields.transpose(0, 1, 3, 4, 2),
        jnp.asarray(band_selector(), BF16),
        score_table.transpose(1, 2, 0),
        score_bias.T,
        value_bias,
        value_table.reshape(GROUPS, OWN, D),
        jnp.asarray(weight_spread(), BF16),
        jnp.asarray(cell_selector(), BF16),
        agg_weight,
        norm_gains,
        qkv_weight,
        proj_weight,
        up_weight,
        down_weight,
        jnp.asarray(quads[0 : 2 * QUAD, 0:HALF], BF16),
        jnp.asarray(quads.T, BF16),
        decode_weight,
        decode_bias.reshape(-1, 128),
    ]
    own = [jax.ShapeDtypeStruct(x.shape, x.dtype) for x in operands]
    own[5] = jax.ShapeDtypeStruct((GROUPS, SLOT, D), BF16)
    out = pl.pallas_call(
        body,
        out_shape=pltpu.VMEM((CELLS // LEV, LEV, VARS * PATCH), BF16),
        in_specs=[pl.BlockSpec(memory_space=pl.ANY)] * len(operands),
        out_specs=pl.BlockSpec(memory_space=pltpu.VMEM),
        scratch_shapes=[pltpu.VMEM(x.shape, x.dtype) for x in own]
        + [
            pltpu.VMEM((PIECES, LOCAL_VARS, PATCH, 512), BF16),
            pltpu.VMEM((GROUPS, 8, SENT_LANES), BF16),
            pltpu.VMEM((GROUPS, 8, SENT_LANES), BF16),
            pltpu.VMEM((PATCH, HEADS, 128), F32),
            pltpu.VMEM((KDIM, HEADS * 128), BF16),
            pltpu.VMEM((HEADS, 128), F32),
            pltpu.VMEM((CELLS, KDIM), F32),
            pltpu.VMEM((HEADS * CELLS, 128), BF16),
            pltpu.VMEM((4, QUAD, D), BF16),
            pltpu.VMEM((4, QUAD, D), BF16),
            pltpu.VMEM((4, QUAD, D), BF16),
            pltpu.VMEM((4, QUAD, D), BF16),
            pltpu.VMEM((2, QUAD, D), BF16),
            pltpu.VMEM((2, QUAD, D), BF16),
            pltpu.SemaphoreType.DMA((GROUPS,)),
            pltpu.SemaphoreType.DMA((GROUPS,)),
            pltpu.SemaphoreType.DMA((8,)),
            pltpu.SemaphoreType.DMA((8,)),
            pltpu.SemaphoreType.DMA((len(operands) + 1,)),
        ],
        compiler_params=pltpu.CompilerParams(
            collective_id=0, has_side_effects=True, vmem_limit_bytes=56 * 1024 * 1024
        ),
        name="forecast_step",
    )(*operands)
    return out.reshape(ROWS, COLS, LEV, VARS * PATCH).transpose(2, 0, 1, 3)


def solution(mesh):
    return jax.shard_map(
        per_device,
        mesh=mesh,
        in_specs=(P(("var", "lat"), None, None, "lon", None),) + (P(),) * 12,
        out_specs=P(None, ("var", "lat"), "lon", None),
        check_vma=False,
    )
```
